32 devices in a mesh: ens: 2 (over y), grid: 4 (over z), pole: 4 (over x, core).
Axes of the slice: x: 2, y: 2, z: 4, core: 2. Of those that a mesh axis runs over, the one named last changes fastest.
Arguments:
- inverse_pool: bfloat16 [8, 2, 4096, 4096], P(('ens', 'pole'), None, 'grid'), parts along dimension 0, may hold values from -6 to 6
- factor_tiles: bfloat16 [8, 4, 2, 10, 256, 256], P(('ens', 'pole'), None, None, None, 'grid'), parts along dimension 0, may hold values from -0.078125 to 0.078125
- diag_inverse: bfloat16 [8, 2, 1024, 256], P(('ens', 'pole'), None, 'grid'), parts along dimension 0, may hold values from -6 to 6
- pole_weight: float32 [4, 2], P('pole'), may hold values from -3 to 3
- ancestors: int32 [4, 10], replicated, may hold values from 0 to 15, all different within a row
Outputs:
- density_panel: float32 [8192, 1024], P(('ens', 'grid'), 'pole'), parts along dimension 0
- density_diagonal: float32 [2048, 256], P(('ens', 'grid')), parts along dimension 0
The draws below stay inside these ranges and needn't reach their ends.
There are 2 independent parts, one for each index of `ens`. The reference program is written for one: setup_inputs(seed, part) draws one part's arguments, and reference() takes and returns one part's arrays. A program takes and returns all parts, laid end to end along the dimension named above; an argument that names none is the same for every part. Nothing has to cross between parts.
Inputs may be any that keep to these rules, and one draw needn't show every extreme that they name: `ancestors`: each row names 10 different ancestor blocks; every one of the 16 blocks is named by some row.
All inputs are finite; a program needn't handle non-finite values.
Results may differ from the reference program's by a relative error of at most 0.0022.
Values may be sent and summed in bfloat16 or wider, within the bound.
No kernel may reach another device: no remote copies, remote signals or barrier semaphores. Data moves between devices by JAX's collectives and lax.ppermute only.
A program may use at most 128 MiB of HBM per device.

```python
import jax
import jax.numpy as jnp
from jax import lax

W = 256
NA = 16
ANC = 10
SUPER = 4
POLES = 4


def block_scale(rng, shape, split, least, largest):
    gain = 1.0
    for position, parts in split:
        steps = jax.random.uniform(jax.random.fold_in(jax.random.fold_in(rng, 6), position), (parts,), jnp.float32, least / len(split), largest / len(split))
        gain = gain * jnp.repeat(jnp.exp(steps), shape[position] // parts).reshape((-1,) + (1,) * (len(shape) - 1 - position))
    return gain


def different_ones(stream_key, rows, amount, top, lift):
    sequence = jax.random.permutation(jax.random.fold_in(stream_key, 1), amount)
    boost = sequence
    for power in range(3):
        boost = boost * boost // amount
    boost = boost * lift // amount
    tickets = jax.random.randint(jax.random.fold_in(stream_key, 2), (rows, amount), 0, 4096) + boost
    sure = jax.random.permutation(jax.random.fold_in(stream_key, 3), rows)[jnp.arange(amount) % rows]
    tickets = jnp.where(jnp.arange(rows)[:, None] == sure[None, :], 1 << 14, tickets)
    priority = tickets * amount + jnp.arange(amount)
    return lax.top_k(priority.astype(jnp.int32), top)[1].astype(jnp.int32)


def scatter_about(rng, shape, deviation, bound, split=(), kind=jnp.bfloat16):
    entries = deviation * jax.random.normal(rng, shape, jnp.float32)
    if split:
        entries = entries * block_scale(rng, shape, split, -0.22, 0.18)
    return jnp.clip(entries, -bound, bound).astype(kind)


def setup_inputs(seed: int = 0, part: int = 0) -> dict:
    seeds = jax.random.split(jax.random.key(seed), 6)
    part_splits = jax.random.split(jax.random.fold_in(seeds[5], part), 6)
    inverse_pool = scatter_about(part_splits[0], (POLES, 2, NA * W, NA * W), 1.0, 6.0, ((0, 4), (2, 4)))
    factor_tiles = scatter_about(part_splits[1], (POLES, SUPER, 2, ANC, W, W), (2 * ANC * W) ** -0.5, 0.078125, ((0, 4), (4, 4)))
    diag_inverse = scatter_about(part_splits[2], (POLES, 2, SUPER * W, W), 1.0, 6.0, ((0, 4), (2, 4)))
    pole_weight = scatter_about(seeds[3], (POLES, 2), POLES ** -0.5, 3.0, ((0, 4),), jnp.float32)
    ancestors = different_ones(seeds[4], SUPER, NA, ANC, 10240)
    return dict(inverse_pool=inverse_pool, factor_tiles=factor_tiles, diag_inverse=diag_inverse, pole_weight=pole_weight, ancestors=ancestors)


def product(left, right):
    return jnp.dot(left, right, precision=lax.Precision.HIGHEST)


def reference(inverse_pool, factor_tiles, diag_inverse, pole_weight, ancestors):
    panel = jnp.zeros((NA * W, SUPER * W), jnp.float32)
    diagonal = jnp.zeros((SUPER * W, W), jnp.float32)
    offsets = jnp.arange(W, dtype=jnp.int32)
    columns_all = (ancestors[:, :, None].astype(jnp.int32) * W + offsets[None, None, :]).reshape(SUPER, ANC * W).astype(jnp.int32)
    for pole_index in range(POLES):
        weight_real = pole_weight[pole_index, 0]
        weight_imag = pole_weight[pole_index, 1]
        for supernode in range(SUPER):
            columns = columns_all[supernode]
            selected = inverse_pool[pole_index][:, columns][:, :, columns].astype(jnp.float32)
            stacked = factor_tiles[pole_index, supernode].astype(jnp.float32).reshape(2, ANC * W, W)
            column_real = -(product(selected[0], stacked[0]) - product(selected[1], stacked[1]))
            column_imag = -(product(selected[0], stacked[1]) + product(selected[1], stacked[0]))
            lower = supernode * W
            panel = panel.at[columns, lower:lower + W].add(weight_real * column_imag + weight_imag * column_real)
            rounded_real = lax.optimization_barrier(column_real.astype(jnp.bfloat16)).astype(jnp.float32)
            rounded_imag = lax.optimization_barrier(column_imag.astype(jnp.bfloat16)).astype(jnp.float32)
            block_tile = diag_inverse[pole_index, :, lower:lower + W].astype(jnp.float32)
            block_real = block_tile[0] - (product(stacked[0].T, rounded_real) - product(stacked[1].T, rounded_imag))
            block_imag = block_tile[1] - (product(stacked[0].T, rounded_imag) + product(stacked[1].T, rounded_real))
            diagonal = diagonal.at[lower:lower + W].add(weight_real * block_imag + weight_imag * block_real)
    return panel, diagonal
```

```python
import functools

import jax
import jax.numpy as jnp
from jax import lax
from jax.experimental import pallas as pl
from jax.experimental.pallas import tpu as pltpu
from jax.sharding import PartitionSpec as P


def plain_product(left, right):
    return jnp.dot(left, right, preferred_element_type=jnp.float32)


def turned_product(left, right):
    return lax.dot_general(
        left, right, (((0,), (0,)), ((), ())), preferred_element_type=jnp.float32
    )


def portion_terms(rows_pair, block_index, offset, listed, factors, weights):
    tile_width = factors.shape[3]
    listed_count = factors.shape[1]
    height = rows_pair.shape[1]
    blocks = rows_pair.shape[2] // tile_width
    matches = listed == block_index

    def compute():
        chosen = rows_pair.reshape(2, height, blocks, tile_width)[:, :, listed, :].reshape(
            2, height, listed_count * tile_width
        )
        stacked = factors.reshape(2, listed_count * tile_width, tile_width)
        part_real = -(plain_product(chosen[0], stacked[0]) - plain_product(chosen[1], stacked[1]))
        part_imag = -(plain_product(chosen[0], stacked[1]) + plain_product(chosen[1], stacked[0]))
        panel_piece = weights[0] * part_imag + weights[1] * part_real
        rounded_real = part_real.astype(jnp.bfloat16)
        rounded_imag = part_imag.astype(jnp.bfloat16)
        position = jnp.sum(jnp.where(matches, jnp.arange(listed_count, dtype=jnp.int32), 0))
        matched = lax.dynamic_slice(
            factors, (jnp.int32(0), position, offset, jnp.int32(0)), (2, 1, height, tile_width)
        )[:, 0]
        diag_real = -(
            turned_product(matched[0], rounded_real) - turned_product(matched[1], rounded_imag)
        )
        diag_imag = -(
            turned_product(matched[0], rounded_imag) + turned_product(matched[1], rounded_real)
        )
        return (panel_piece, weights[0] * diag_imag + weights[1] * diag_real)

    def skipped():
        return (
            jnp.zeros((height, tile_width), jnp.float32),
            jnp.zeros((tile_width, tile_width), jnp.float32),
        )

    return lax.cond(jnp.any(matches), compute, skipped)


def rows_terms(rows_pair, row_first, listed, factors, weights):
    tile_width = factors.shape[3]
    height = rows_pair.shape[1]
    piece_rows = min(height, tile_width)
    panels = []
    diag_total = jnp.zeros((tile_width, tile_width), jnp.float32)
    for portion in range(height // piece_rows):
        row_start = row_first + portion * piece_rows
        panel_piece, diag_piece = portion_terms(
            rows_pair[:, portion * piece_rows : (portion + 1) * piece_rows],
            row_start // tile_width,
            row_start % tile_width,
            listed,
            factors,
            weights,
        )
        panels.append(panel_piece)
        diag_total = diag_total + diag_piece
    return (jnp.concatenate(panels, axis=0), diag_total)


def shards_any(inverse_pool, factor_tiles, diag_inverse, pole_weight, ancestors):
    device_index = lax.axis_index("grid")
    rows_here = inverse_pool.shape[2]
    supers = factor_tiles.shape[1]
    tile_width = factor_tiles.shape[5]
    row_slab = inverse_pool[0]
    weights = (pole_weight[0, 0], pole_weight[0, 1])
    row_first = device_index * rows_here
    own_panels = []
    diag_terms = []
    for supernode in range(supers):
        factors = lax.all_gather(factor_tiles[0, supernode], "grid", axis=2, tiled=True)
        listed = ancestors[supernode]
        own_panel, own_diag = rows_terms(row_slab, row_first, listed, factors, weights)
        diag_terms.append(own_diag)
        own_panels.append(own_panel)
    panel_rows = jnp.concatenate(own_panels, axis=1)
    panel_share = lax.psum_scatter(panel_rows, "pole", scatter_dimension=1, tiled=True)
    diag_term = jnp.stack(diag_terms, axis=0).reshape(supers * tile_width, tile_width)
    diag_local = diag_inverse[0]
    local_block = weights[0] * diag_local[1].astype(jnp.float32) + weights[1] * diag_local[
        0
    ].astype(jnp.float32)
    share_rows = local_block.shape[0]
    placed = lax.dynamic_update_slice(
        jnp.zeros_like(diag_term), local_block, (device_index * share_rows, jnp.int32(0))
    )
    spread = lax.psum_scatter(diag_term + placed, ("grid", "pole"), scatter_dimension=0, tiled=True)
    diag_share = lax.all_gather(spread, "pole", axis=0, tiled=True)
    return (panel_share, diag_share)


def supernode_kernel(
    supernode,
    listed_ref,
    place_ref,
    weight_ref,
    pool_ref,
    tiles_ref,
    swap_ref,
    mid_near_ref,
    mid_far_ref,
    end_near_ref,
    end_far_ref,
    local_ref,
    panel_ref,
    diag_ref,
    factors,
    rows,
    factor_sems,
    row_sems,
):
    width = panel_ref.shape[1]
    listed_count = factors.shape[0]
    slices = panel_ref.shape[0] // width
    depth = tiles_ref.shape[4]
    place = place_ref[0]
    edge = place_ref[1]
    first_half = place_ref[2]
    odd = lax.rem(place, 2)

    position = []
    for part in range(slices):
        block = place * slices + part
        found = jnp.int32(-1)
        for item in range(listed_count):
            found = jnp.where(listed_ref[supernode, item] == block, jnp.int32(item), found)
        position.append(found)

    def factor_copies(source, slot, sem):
        start = pl.multiple_of(slot * depth, depth)
        return [
            pltpu.make_async_copy(
                source.at[part],
                factors.at[:, pl.ds(start, depth), pl.ds(part * width, width)],
                factor_sems.at[sem, part],
            )
            for part in range(2)
        ]

    near_slot = 1 - first_half
    pieces = [
        (tiles_ref.at[0, supernode], odd, None),
        (swap_ref, 1 - odd, None),
        (mid_near_ref, near_slot + 2 * first_half, 0),
        (end_near_ref, near_slot + 2 * first_half, 1),
        (mid_far_ref, 1 - near_slot + 2 * first_half, 0),
        (end_far_ref, 1 - near_slot + 2 * first_half, 1),
    ]
    own_base = 2 * (1 - first_half)
    plan = []
    for number, (source, slot, role) in enumerate(pieces):
        where = slot + own_base if role is None else slot
        plan.append((factor_copies(source, where, number), role))

    def each_piece(action):
        for copies, role in plan:
            if role is None:
                for copy in copies:
                    action(copy)
            else:

                @pl.when(edge == role)
                def _(copies=copies):
                    for copy in copies:
                        action(copy)

    each_piece(lambda copy: copy.start())
    for part in range(slices):

        @pl.when(position[part] >= 0)
        def _(part=part):
            for item in range(listed_count):
                column = pl.multiple_of(listed_ref[supernode, item] * width, width)
                pltpu.make_async_copy(
                    pool_ref.at[0, :, pl.ds(part * width, width), pl.ds(column, width)],
                    rows.at[part, :, :, pl.ds(item * width, width)],
                    row_sems.at[part],
                ).start()

    weight_real = weight_ref[0, 0]
    weight_imag = weight_ref[0, 1]
    here = (place == supernode).astype(jnp.float32)
    diag_ref[...] = here * (
        weight_real * local_ref[0, 1].astype(jnp.float32)
        + weight_imag * local_ref[0, 0].astype(jnp.float32)
    )
    each_piece(lambda copy: copy.wait())

    for part in range(slices):
        panel_rows = pl.ds(part * width, width)

        @pl.when(position[part] < 0)
        def _(panel_rows=panel_rows):
            panel_ref[panel_rows, :] = jnp.zeros((width, width), jnp.float32)

        @pl.when(position[part] >= 0)
        def _(part=part, panel_rows=panel_rows):
            pltpu.make_async_copy(
                pool_ref.at[0, :, pl.ds(0, width), pl.ds(0, listed_count * width)],
                rows.at[part],
                row_sems.at[part],
            ).wait()
            stacked = factors[...].reshape(listed_count * 4 * depth, 2 * width)
            by_real = plain_product(rows[part, 0], stacked)
            by_imag = plain_product(rows[part, 1], stacked)
            real = -(by_real[:, :width] - by_imag[:, width:])
            imag = -(by_real[:, width:] + by_imag[:, :width])
            panel_ref[panel_rows, :] = weight_real * imag + weight_imag * real
            both = jnp.concatenate(
                [real.astype(jnp.bfloat16), imag.astype(jnp.bfloat16)], axis=1
            )
            crossed = turned_product(factors[position[part]], both)
            diag_real = -(crossed[:width, :width] - crossed[width:, width:])
            diag_imag = -(crossed[:width, width:] + crossed[width:, :width])
            diag_ref[...] += weight_real * diag_imag + weight_imag * diag_real


def supernode_terms(
    supernode, listed, places, weights, pool, tiles, swap, mid_near, mid_far, end_near, end_far, local
):
    width = tiles.shape[5]
    depth = tiles.shape[4]
    listed_count = tiles.shape[3]
    height = pool.shape[2]
    slices = height // width
    anywhere = pl.BlockSpec(memory_space=pl.ANY)
    scalars = pl.BlockSpec(memory_space=pltpu.SMEM)
    whole = pl.BlockSpec(memory_space=pltpu.VMEM)
    return pl.pallas_call(
        functools.partial(supernode_kernel, supernode),
        out_shape=(
            jax.ShapeDtypeStruct((height, width), jnp.float32),
            jax.ShapeDtypeStruct((width, width), jnp.float32),
        ),
        in_specs=[scalars] * 3 + [anywhere] * 7 + [whole],
        out_specs=(whole, whole),
        scratch_shapes=[
            pltpu.VMEM((listed_count, 4 * depth, 2 * width), jnp.bfloat16),
            pltpu.VMEM((slices, 2, width, listed_count * width), jnp.bfloat16),
            pltpu.SemaphoreType.DMA((6, 2)),
            pltpu.SemaphoreType.DMA((slices,)),
        ],
        compiler_params=pltpu.CompilerParams(vmem_limit_bytes=40 * 1024 * 1024),
        cost_estimate=pl.CostEstimate(
            flops=8 * height * width * width * listed_count,
            bytes_accessed=6 * height * width * listed_count,
            transcendentals=0,
        ),
        name=f"supernode_{supernode}",
    )(listed, places, weights, pool, tiles, swap, mid_near, mid_far, end_near, end_far, local)


def shards_line(inverse_pool, factor_tiles, diag_inverse, pole_weight, ancestors):
    supers = factor_tiles.shape[1]
    width = factor_tiles.shape[5]
    place = lax.axis_index("grid")
    pole = lax.axis_index("pole")
    chip = pole // 2
    core = pole % 2
    edge = jnp.logical_or(place == 0, place == 3)
    first_half = (place < 2).astype(jnp.int32)
    places = jnp.stack([place, edge.astype(jnp.int32), first_half]).astype(jnp.int32)

    pairs_z = [(0, 1), (1, 0), (2, 3), (3, 2)]
    middle_z = [(1, 2), (2, 1)]
    outward_z = [(1, 0), (2, 3)]
    across_x = [(0, 2), (2, 0), (1, 3), (3, 1)]
    groups = ((0, 3), (1, 2))

    terms = {}
    for group in groups:
        for k in group:
            own = factor_tiles[0, k]
            swap = lax.ppermute(own, "grid", pairs_z)
            mid_near = lax.ppermute(own, "grid", middle_z)
            mid_far = lax.ppermute(swap, "grid", middle_z)
            end_near = lax.ppermute(mid_near, "grid", outward_z)
            end_far = lax.ppermute(mid_far, "grid", outward_z)
            terms[k] = supernode_terms(
                k, ancestors, places, pole_weight, inverse_pool, factor_tiles,
                swap, mid_near, mid_far, end_near, end_far, diag_inverse,
            )

    panel_sums = []
    diag_sums = []
    quarter = width // 4
    for low, high in groups:
        panel_low, diag_low = terms[low]
        panel_high, diag_high = terms[high]
        sent = jnp.where(chip == 0, panel_high, panel_low).astype(jnp.bfloat16)
        kept = jnp.where(chip == 0, panel_low, panel_high)
        chip_sum = kept + lax.ppermute(sent, "pole", across_x).astype(jnp.float32)
        to_owner = [(low + 1 - 2 * (low % 2), low), (high + 1 - 2 * (high % 2), high)]
        panel_sums.append(chip_sum + lax.ppermute(chip_sum, "pole", to_owner))
        both = jnp.stack([diag_low, diag_high])
        half_rows = 2 * quarter
        sent = lax.dynamic_slice_in_dim(both, (1 - chip) * half_rows, half_rows, 1)
        kept = lax.dynamic_slice_in_dim(both, chip * half_rows, half_rows, 1)
        both = kept + lax.ppermute(sent, "pole", across_x)
        sent = lax.dynamic_slice_in_dim(both, (1 - core) * quarter, quarter, 1)
        kept = lax.dynamic_slice_in_dim(both, core * quarter, quarter, 1)
        both = kept + lax.ppermute(sent, "pole", pairs_z)
        total = jnp.where(place == high, both[1], both[0])
        for shift in range(1, 4):
            target = (place + shift) % 4
            sent = jnp.where(target == high, both[1], both[0])
            total = total + lax.ppermute(
                sent, "grid", [((t - shift) % 4, t) for t in (low, high)]
            )
        diag_sums.append(total)

    in_first = jnp.logical_or(pole == groups[0][0], pole == groups[0][1])
    panel_share = jnp.where(in_first, panel_sums[0], panel_sums[1])
    in_first = jnp.logical_or(place == groups[0][0], place == groups[0][1])
    own = jnp.where(in_first, diag_sums[0], diag_sums[1])
    other = lax.ppermute(own, "pole", pairs_z)
    half = jnp.where(
        core == 0, jnp.concatenate([own, other]), jnp.concatenate([other, own])
    )
    other = lax.ppermute(half, "pole", across_x)
    diag_share = jnp.where(
        chip == 0, jnp.concatenate([half, other]), jnp.concatenate([other, half])
    )
    return (panel_share, diag_share)


def solution(mesh):
    in_specs = (
        P(("ens", "pole"), None, "grid", None),
        P(("ens", "pole"), None, None, None, "grid", None),
        P(("ens", "pole"), None, "grid", None),
        P("pole", None),
        P(),
    )
    out_specs = (P(("ens", "grid"), "pole"), P(("ens", "grid"), None))

    def shards(inverse_pool, factor_tiles, diag_inverse, pole_weight, ancestors):
        groups = mesh.shape["grid"]
        poles = mesh.shape["pole"]
        supers = factor_tiles.shape[1]
        width = factor_tiles.shape[5]
        line = (
            groups == 4
            and poles == 4
            and supers == 4
            and factor_tiles.shape[4] * groups == width
            and inverse_pool.shape[2] % width == 0
            and diag_inverse.shape[2] == width
            and width % 256 == 0
        )
        chosen = shards_line if line else shards_any
        return chosen(inverse_pool, factor_tiles, diag_inverse, pole_weight, ancestors)

    return jax.shard_map(shards, mesh=mesh, in_specs=in_specs, out_specs=out_specs, check_vma=False)
```

```python
import functools

import jax
import jax.numpy as jnp
from jax import lax
from jax.experimental import pallas as pl
from jax.experimental.pallas import tpu as pltpu
from jax.sharding import PartitionSpec as P


def plain_product(left, right):
    return jnp.dot(left, right, preferred_element_type=jnp.float32)


def turned_product(left, right):
    return lax.dot_general(
        left, right, (((0,), (0,)), ((), ())), preferred_element_type=jnp.float32
    )


def portion_terms(rows_pair, block_index, offset, listed, factors, weights):
    tile_width = factors.shape[3]
    listed_count = factors.shape[1]
    height = rows_pair.shape[1]
    blocks = rows_pair.shape[2] // tile_width
    matches = listed == block_index

    def compute():
        chosen = rows_pair.reshape(2, height, blocks, tile_width)[:, :, listed, :].reshape(
            2, height, listed_count * tile_width
        )
        stacked = factors.reshape(2, listed_count * tile_width, tile_width)
        part_real = -(plain_product(chosen[0], stacked[0]) - plain_product(chosen[1], stacked[1]))
        part_imag = -(plain_product(chosen[0], stacked[1]) + plain_product(chosen[1], stacked[0]))
        panel_piece = weights[0] * part_imag + weights[1] * part_real
        rounded_real = part_real.astype(jnp.bfloat16)
        rounded_imag = part_imag.astype(jnp.bfloat16)
        position = jnp.sum(jnp.where(matches, jnp.arange(listed_count, dtype=jnp.int32), 0))
        matched = lax.dynamic_slice(
            factors, (jnp.int32(0), position, offset, jnp.int32(0)), (2, 1, height, tile_width)
        )[:, 0]
        diag_real = -(
            turned_product(matched[0], rounded_real) - turned_product(matched[1], rounded_imag)
        )
        diag_imag = -(
            turned_product(matched[0], rounded_imag) + turned_product(matched[1], rounded_real)
        )
        return (panel_piece, weights[0] * diag_imag + weights[1] * diag_real)

    def skipped():
        return (
            jnp.zeros((height, tile_width), jnp.float32),
            jnp.zeros((tile_width, tile_width), jnp.float32),
        )

    return lax.cond(jnp.any(matches), compute, skipped)


def rows_terms(rows_pair, row_first, listed, factors, weights):
    tile_width = factors.shape[3]
    height = rows_pair.shape[1]
    piece_rows = min(height, tile_width)
    panels = []
    diag_total = jnp.zeros((tile_width, tile_width), jnp.float32)
    for portion in range(height // piece_rows):
        row_start = row_first + portion * piece_rows
        panel_piece, diag_piece = portion_terms(
            rows_pair[:, portion * piece_rows : (portion + 1) * piece_rows],
            row_start // tile_width,
            row_start % tile_width,
            listed,
            factors,
            weights,
        )
        panels.append(panel_piece)
        diag_total = diag_total + diag_piece
    return (jnp.concatenate(panels, axis=0), diag_total)


def shards_any(inverse_pool, factor_tiles, diag_inverse, pole_weight, ancestors):
    device_index = lax.axis_index("grid")
    rows_here = inverse_pool.shape[2]
    supers = factor_tiles.shape[1]
    tile_width = factor_tiles.shape[5]
    row_slab = inverse_pool[0]
    weights = (pole_weight[0, 0], pole_weight[0, 1])
    row_first = device_index * rows_here
    own_panels = []
    diag_terms = []
    for supernode in range(supers):
        factors = lax.all_gather(factor_tiles[0, supernode], "grid", axis=2, tiled=True)
        listed = ancestors[supernode]
        own_panel, own_diag = rows_terms(row_slab, row_first, listed, factors, weights)
        diag_terms.append(own_diag)
        own_panels.append(own_panel)
    panel_rows = jnp.concatenate(own_panels, axis=1)
    panel_share = lax.psum_scatter(panel_rows, "pole", scatter_dimension=1, tiled=True)
    diag_term = jnp.stack(diag_terms, axis=0).reshape(supers * tile_width, tile_width)
    diag_local = diag_inverse[0]
    local_block = weights[0] * diag_local[1].astype(jnp.float32) + weights[1] * diag_local[
        0
    ].astype(jnp.float32)
    share_rows = local_block.shape[0]
    placed = lax.dynamic_update_slice(
        jnp.zeros_like(diag_term), local_block, (device_index * share_rows, jnp.int32(0))
    )
    spread = lax.psum_scatter(diag_term + placed, ("grid", "pole"), scatter_dimension=0, tiled=True)
    diag_share = lax.all_gather(spread, "pole", axis=0, tiled=True)
    return (panel_share, diag_share)


def supernode_kernel(
    supernode,
    listed_ref,
    place_ref,
    weight_ref,
    pool_ref,
    tiles_ref,
    swap_ref,
    mid_near_ref,
    mid_far_ref,
    end_near_ref,
    end_far_ref,
    local_ref,
    panel_ref,
    diag_ref,
    factors,
    rows,
    factor_sems,
    row_sems,
):
    width = panel_ref.shape[1]
    listed_count = factors.shape[0]
    slices = panel_ref.shape[0] // width
    depth = tiles_ref.shape[4]
    place = place_ref[0]
    edge = place_ref[1]
    first_half = place_ref[2]
    odd = lax.rem(place, 2)

    position = []
    for part in range(slices):
        block = place * slices + part
        found = jnp.int32(-1)
        for item in range(listed_count):
            found = jnp.where(listed_ref[supernode, item] == block, jnp.int32(item), found)
        position.append(found)

    def factor_copies(source, slot, sem):
        start = pl.multiple_of(slot * depth, depth)
        return [
            pltpu.make_async_copy(
                source.at[part],
                factors.at[:, pl.ds(start, depth), pl.ds(part * width, width)],
                factor_sems.at[sem, part],
            )
            for part in range(2)
        ]

    near_slot = 1 - first_half
    pieces = [
        (tiles_ref.at[0, supernode], odd, None),
        (swap_ref, 1 - odd, None),
        (mid_near_ref, near_slot + 2 * first_half, 0),
        (end_near_ref, near_slot + 2 * first_half, 1),
        (mid_far_ref, 1 - near_slot + 2 * first_half, 0),
        (end_far_ref, 1 - near_slot + 2 * first_half, 1),
    ]
    own_base = 2 * (1 - first_half)
    plan = []
    for number, (source, slot, role) in enumerate(pieces):
        where = slot + own_base if role is None else slot
        plan.append((factor_copies(source, where, number), role))

    def each_piece(action):
        for copies, role in plan:
            if role is None:
                for copy in copies:
                    action(copy)
            else:

                @pl.when(edge == role)
                def _(copies=copies):
                    for copy in copies:
                        action(copy)

    each_piece(lambda copy: copy.start())
    for part in range(slices):

        @pl.when(position[part] >= 0)
        def _(part=part):
            for item in range(listed_count):
                column = pl.multiple_of(listed_ref[supernode, item] * width, width)
                pltpu.make_async_copy(
                    pool_ref.at[0, :, pl.ds(part * width, width), pl.ds(column, width)],
                    rows.at[part, :, :, pl.ds(item * width, width)],
                    row_sems.at[part],
                ).start()

    weight_real = weight_ref[0, 0]
    weight_imag = weight_ref[0, 1]
    here = (place == supernode).astype(jnp.float32)
    diag_ref[...] = here * (
        weight_real * local_ref[0, 1].astype(jnp.float32)
        + weight_imag * local_ref[0, 0].astype(jnp.float32)
    )
    each_piece(lambda copy: copy.wait())

    for part in range(slices):
        panel_rows = pl.ds(part * width, width)

        @pl.when(position[part] < 0)
        def _(panel_rows=panel_rows):
            panel_ref[panel_rows, :] = jnp.zeros((width, width), jnp.float32)

        @pl.when(position[part] >= 0)
        def _(part=part, panel_rows=panel_rows):
            pltpu.make_async_copy(
                pool_ref.at[0, :, pl.ds(0, width), pl.ds(0, listed_count * width)],
                rows.at[part],
                row_sems.at[part],
            ).wait()
            stacked = factors[...].reshape(listed_count * 4 * depth, 2 * width)
            by_real = plain_product(rows[part, 0], stacked)
            by_imag = plain_product(rows[part, 1], stacked)
            real = -(by_real[:, :width] - by_imag[:, width:])
            imag = -(by_real[:, width:] + by_imag[:, :width])
            panel_ref[panel_rows, :] = weight_real * imag + weight_imag * real
            both = jnp.concatenate(
                [real.astype(jnp.bfloat16), imag.astype(jnp.bfloat16)], axis=1
            )
            crossed = turned_product(factors[position[part]], both)
            diag_real = -(crossed[:width, :width] - crossed[width:, width:])
            diag_imag = -(crossed[:width, width:] + crossed[width:, :width])
            diag_ref[...] += weight_real * diag_imag + weight_imag * diag_real


def supernode_terms(
    supernode, listed, places, weights, pool, tiles, swap, mid_near, mid_far, end_near, end_far, local
):
    width = tiles.shape[5]
    depth = tiles.shape[4]
    listed_count = tiles.shape[3]
    height = pool.shape[2]
    slices = height // width
    anywhere = pl.BlockSpec(memory_space=pl.ANY)
    scalars = pl.BlockSpec(memory_space=pltpu.SMEM)
    whole = pl.BlockSpec(memory_space=pltpu.VMEM)
    return pl.pallas_call(
        functools.partial(supernode_kernel, supernode),
        out_shape=(
            jax.ShapeDtypeStruct((height, width), jnp.float32),
            jax.ShapeDtypeStruct((width, width), jnp.float32),
        ),
        in_specs=[scalars] * 3 + [anywhere] * 7 + [whole],
        out_specs=(whole, whole),
        scratch_shapes=[
            pltpu.VMEM((listed_count, 4 * depth, 2 * width), jnp.bfloat16),
            pltpu.VMEM((slices, 2, width, listed_count * width), jnp.bfloat16),
            pltpu.SemaphoreType.DMA((6, 2)),
            pltpu.SemaphoreType.DMA((slices,)),
        ],
        compiler_params=pltpu.CompilerParams(vmem_limit_bytes=40 * 1024 * 1024),
        cost_estimate=pl.CostEstimate(
            flops=8 * height * width * width * listed_count,
            bytes_accessed=6 * height * width * listed_count,
            transcendentals=0,
        ),
        name=f"supernode_{supernode}",
    )(listed, places, weights, pool, tiles, swap, mid_near, mid_far, end_near, end_far, local)


def shards_line(inverse_pool, factor_tiles, diag_inverse, pole_weight, ancestors):
    supers = factor_tiles.shape[1]
    width = factor_tiles.shape[5]
    place = lax.axis_index("grid")
    pole = lax.axis_index("pole")
    chip = pole // 2
    core = pole % 2
    edge = jnp.logical_or(place == 0, place == 3)
    first_half = (place < 2).astype(jnp.int32)
    places = jnp.stack([place, edge.astype(jnp.int32), first_half]).astype(jnp.int32)

    pairs_z = [(0, 1), (1, 0), (2, 3), (3, 2)]
    middle_z = [(1, 2), (2, 1)]
    outward_z = [(1, 0), (2, 3)]
    across_x = [(0, 2), (2, 0), (1, 3), (3, 1)]
    groups = ((0, 3), (1, 2))

    quarter = width // 4
    listed = ancestors
    panel_sums = []
    diag_sums = []
    for number, (low, high) in enumerate(groups):
        terms = {}
        for k in (low, high):
            own = factor_tiles[0, k]
            swap = lax.ppermute(own, "grid", pairs_z)
            mid_near = lax.ppermute(own, "grid", middle_z)
            mid_far = lax.ppermute(swap, "grid", middle_z)
            end_near = lax.ppermute(mid_near, "grid", outward_z)
            end_far = lax.ppermute(mid_far, "grid", outward_z)
            terms[k] = supernode_terms(
                k, listed, places, pole_weight, inverse_pool, factor_tiles,
                swap, mid_near, mid_far, end_near, end_far, diag_inverse,
            )
        panel_low, diag_low = terms[low]
        panel_high, diag_high = terms[high]
        sent = jnp.where(chip == 0, panel_high, panel_low).astype(jnp.bfloat16)
        kept = jnp.where(chip == 0, panel_low, panel_high)
        chip_sum = kept + lax.ppermute(sent, "pole", across_x).astype(jnp.float32)
        to_owner = [(low + 1 - 2 * (low % 2), low), (high + 1 - 2 * (high % 2), high)]
        panel_sum = chip_sum + lax.ppermute(chip_sum, "pole", to_owner)
        both = jnp.stack([diag_low, diag_high])
        half_rows = 2 * quarter
        sent = lax.dynamic_slice_in_dim(both, (1 - core) * half_rows, half_rows, 1)
        kept = lax.dynamic_slice_in_dim(both, core * half_rows, half_rows, 1)
        both = kept + lax.ppermute(sent, "pole", pairs_z)
        sent = lax.dynamic_slice_in_dim(both, (1 - chip) * quarter, quarter, 1)
        kept = lax.dynamic_slice_in_dim(both, chip * quarter, quarter, 1)
        both = kept + lax.ppermute(sent, "pole", across_x)
        total = jnp.where(place == high, both[1], both[0])
        for shift in range(1, 4):
            target = (place + shift) % 4
            sent = jnp.where(target == high, both[1], both[0])
            total = total + lax.ppermute(
                sent, "grid", [((t - shift) % 4, t) for t in (low, high)]
            )
        if number == 0:
            listed, panel_sum, total = lax.optimization_barrier((listed, panel_sum, total))
        panel_sums.append(panel_sum)
        diag_sums.append(total)

    in_first = jnp.logical_or(pole == groups[0][0], pole == groups[0][1])
    panel_share = jnp.where(in_first, panel_sums[0], panel_sums[1])
    in_first = jnp.logical_or(place == groups[0][0], place == groups[0][1])
    own = jnp.where(in_first, diag_sums[0], diag_sums[1])
    other = lax.ppermute(own, "pole", across_x)
    half = jnp.where(
        chip == 0, jnp.concatenate([own, other]), jnp.concatenate([other, own])
    )
    other = lax.ppermute(half, "pole", pairs_z)
    diag_share = jnp.where(
        core == 0, jnp.concatenate([half, other]), jnp.concatenate([other, half])
    )
    return (panel_share, diag_share)


def solution(mesh):
    in_specs = (
        P(("ens", "pole"), None, "grid", None),
        P(("ens", "pole"), None, None, None, "grid", None),
        P(("ens", "pole"), None, "grid", None),
        P("pole", None),
        P(),
    )
    out_specs = (P(("ens", "grid"), "pole"), P(("ens", "grid"), None))

    def shards(inverse_pool, factor_tiles, diag_inverse, pole_weight, ancestors):
        groups = mesh.shape["grid"]
        poles = mesh.shape["pole"]
        supers = factor_tiles.shape[1]
        width = factor_tiles.shape[5]
        line = (
            groups == 4
            and poles == 4
            and supers == 4
            and factor_tiles.shape[4] * groups == width
            and inverse_pool.shape[2] % width == 0
            and diag_inverse.shape[2] == width
            and width % 256 == 0
        )
        chosen = shards_line if line else shards_any
        return chosen(inverse_pool, factor_tiles, diag_inverse, pole_weight, ancestors)

    return jax.shard_map(shards, mesh=mesh, in_specs=in_specs, out_specs=out_specs, check_vma=False)
```

```python
import functools

import jax
import jax.numpy as jnp
from jax import lax
from jax.experimental import pallas as pl
from jax.experimental.pallas import tpu as pltpu
from jax.sharding import PartitionSpec as P


def plain_product(left, right):
    return jnp.dot(left, right, preferred_element_type=jnp.float32)


def turned_product(left, right):
    return lax.dot_general(
        left, right, (((0,), (0,)), ((), ())), preferred_element_type=jnp.float32
    )


def portion_terms(rows_pair, block_index, offset, listed, factors, weights):
    tile_width = factors.shape[3]
    listed_count = factors.shape[1]
    height = rows_pair.shape[1]
    blocks = rows_pair.shape[2] // tile_width
    matches = listed == block_index

    def compute():
        chosen = rows_pair.reshape(2, height, blocks, tile_width)[:, :, listed, :].reshape(
            2, height, listed_count * tile_width
        )
        stacked = factors.reshape(2, listed_count * tile_width, tile_width)
        part_real = -(plain_product(chosen[0], stacked[0]) - plain_product(chosen[1], stacked[1]))
        part_imag = -(plain_product(chosen[0], stacked[1]) + plain_product(chosen[1], stacked[0]))
        panel_piece = weights[0] * part_imag + weights[1] * part_real
        rounded_real = part_real.astype(jnp.bfloat16)
        rounded_imag = part_imag.astype(jnp.bfloat16)
        position = jnp.sum(jnp.where(matches, jnp.arange(listed_count, dtype=jnp.int32), 0))
        matched = lax.dynamic_slice(
            factors, (jnp.int32(0), position, offset, jnp.int32(0)), (2, 1, height, tile_width)
        )[:, 0]
        diag_real = -(
            turned_product(matched[0], rounded_real) - turned_product(matched[1], rounded_imag)
        )
        diag_imag = -(
            turned_product(matched[0], rounded_imag) + turned_product(matched[1], rounded_real)
        )
        return (panel_piece, weights[0] * diag_imag + weights[1] * diag_real)

    def skipped():
        return (
            jnp.zeros((height, tile_width), jnp.float32),
            jnp.zeros((tile_width, tile_width), jnp.float32),
        )

    return lax.cond(jnp.any(matches), compute, skipped)


def rows_terms(rows_pair, row_first, listed, factors, weights):
    tile_width = factors.shape[3]
    height = rows_pair.shape[1]
    piece_rows = min(height, tile_width)
    panels = []
    diag_total = jnp.zeros((tile_width, tile_width), jnp.float32)
    for portion in range(height // piece_rows):
        row_start = row_first + portion * piece_rows
        panel_piece, diag_piece = portion_terms(
            rows_pair[:, portion * piece_rows : (portion + 1) * piece_rows],
            row_start // tile_width,
            row_start % tile_width,
            listed,
            factors,
            weights,
        )
        panels.append(panel_piece)
        diag_total = diag_total + diag_piece
    return (jnp.concatenate(panels, axis=0), diag_total)


def shards_any(inverse_pool, factor_tiles, diag_inverse, pole_weight, ancestors):
    device_index = lax.axis_index("grid")
    rows_here = inverse_pool.shape[2]
    supers = factor_tiles.shape[1]
    tile_width = factor_tiles.shape[5]
    row_slab = inverse_pool[0]
    weights = (pole_weight[0, 0], pole_weight[0, 1])
    row_first = device_index * rows_here
    own_panels = []
    diag_terms = []
    for supernode in range(supers):
        factors = lax.all_gather(factor_tiles[0, supernode], "grid", axis=2, tiled=True)
        listed = ancestors[supernode]
        own_panel, own_diag = rows_terms(row_slab, row_first, listed, factors, weights)
        diag_terms.append(own_diag)
        own_panels.append(own_panel)
    panel_rows = jnp.concatenate(own_panels, axis=1)
    panel_share = lax.psum_scatter(panel_rows, "pole", scatter_dimension=1, tiled=True)
    diag_term = jnp.stack(diag_terms, axis=0).reshape(supers * tile_width, tile_width)
    diag_local = diag_inverse[0]
    local_block = weights[0] * diag_local[1].astype(jnp.float32) + weights[1] * diag_local[
        0
    ].astype(jnp.float32)
    share_rows = local_block.shape[0]
    placed = lax.dynamic_update_slice(
        jnp.zeros_like(diag_term), local_block, (device_index * share_rows, jnp.int32(0))
    )
    spread = lax.psum_scatter(diag_term + placed, ("grid", "pole"), scatter_dimension=0, tiled=True)
    diag_share = lax.all_gather(spread, "pole", axis=0, tiled=True)
    return (panel_share, diag_share)


PAIRS_Z = [(0, 1), (1, 0), (2, 3), (3, 2)]
MIDDLE_Z = [(1, 2), (2, 1)]
OUTWARD_Z = [(1, 0), (2, 3)]
INWARD_Z = [(0, 1), (3, 2)]
ACROSS_X = [(0, 2), (2, 0), (1, 3), (3, 1)]
CHUNKS = ((0, 3), (1,), (2,))


ANYWHERE = pl.BlockSpec(memory_space=pl.ANY)
STAYING = pl.BlockSpec(memory_space=pltpu.MemorySpace.HBM)
SCALARS = pl.BlockSpec(memory_space=pltpu.SMEM)
WHOLE = pl.BlockSpec(memory_space=pltpu.VMEM)


def near_rows_kernel(table_ref, place_ref, tiles_ref, out_ref, sems):
    supers = out_ref.shape[0]
    slices = out_ref.shape[2]
    end_block = place_ref[3]

    def each(action):
        for k in range(supers):
            for part in range(slices):
                found = table_ref[k, end_block + part]

                @pl.when(found >= 0)
                def _(k=k, part=part, found=found):
                    action(
                        pltpu.make_async_copy(
                            tiles_ref.at[0, k, :, found],
                            out_ref.at[k, :, part],
                            sems.at[k, part],
                        )
                    )

    each(lambda copy: copy.start())
    each(lambda copy: copy.wait())


def pack_columns_kernel(depth, width, place_ref, pool_ref, out_ref):
    first_half = place_ref[2]
    blocks = pool_ref.shape[3] // width

    @pl.when(place_ref[1] == 1)
    def _():
        for offset, flag in ((depth, 1), (2 * depth, 0)):

            @pl.when(first_half == flag)
            def _(offset=offset):
                for part in range(2):
                    out_ref[part] = jnp.concatenate(
                        [
                            pool_ref[0, part, :, q * width + offset : q * width + offset + depth]
                            for q in range(blocks)
                        ],
                        axis=1,
                    )


def packed_columns(places, pool, depth, width, half, halves):
    height = pool.shape[2] // halves
    slices = pool.shape[2] // width
    tile = min(height, width)
    steps = height // tile
    groups = pool.shape[3] // (slices * width) - 1
    return pl.pallas_call(
        functools.partial(pack_columns_kernel, depth, width),
        out_shape=jax.ShapeDtypeStruct((2, height, groups * slices * depth), pool.dtype),
        grid_spec=pltpu.PrefetchScalarGridSpec(
            num_scalar_prefetch=1,
            grid=(steps, groups),
            in_specs=[
                pl.BlockSpec(
                    (1, 2, tile, slices * width),
                    lambda i, j, place: (0, 0, (half * steps + i) * place[1], (j + place[2]) * place[1]),
                )
            ],
            out_specs=pl.BlockSpec(
                (2, tile, slices * depth), lambda i, j, place: (0, i * place[1], j * place[1])
            ),
        ),
        cost_estimate=pl.CostEstimate(
            flops=0, bytes_accessed=3 * pool.shape[3] * height * 2, transcendentals=0
        ),
    )(places, pool)


def supernode_kernel(
    supernode,
    item_in_chunk,
    role,
    fresh,
    lent_item,
    table_ref,
    listed_ref,
    place_ref,
    weight_ref,
    pool_ref,
    tiles_ref,
    partner_ref,
    far_near_ref,
    far_far_ref,
    local_ref,
    *refs,
):
    columns_ref = None
    if lent_item is not None:
        columns_ref, *refs = refs
    diag_in_ref = refs[0] if fresh else refs[2]
    refs = refs[1:] if fresh else refs[3:]
    (
        sent_ref,
        kept_ref,
        diag_ref,
        factors,
        rows,
        out16,
        out32,
        total,
        columns,
        factor_sems,
        near_sems,
        row_sems,
        out_sems,
        diag_sem,
        column_sem,
    ) = refs
    width = total.shape[0]
    listed_count = factors.shape[0]
    slices = rows.shape[0]
    depth = tiles_ref.shape[4]
    place = place_ref[0]
    first_half = place_ref[2]
    end_block = place_ref[3]
    keeps = place_ref[5] == supernode // 2
    odd = lax.rem(place, 2)

    own_base = 2 * (1 - first_half)
    far_base = 2 * first_half
    near_slot = 1 - first_half
    near_start = pl.multiple_of((1 - odd + own_base) * depth, depth)
    pieces = [
        (tiles_ref.at[0, supernode], odd + own_base),
        (far_near_ref.at[item_in_chunk], near_slot + far_base),
        (far_far_ref.at[item_in_chunk], 1 - near_slot + far_base),
    ]
    if not role:
        pieces.append((partner_ref.at[item_in_chunk], 1 - odd + own_base))

    def each_piece(action):
        for number, (source, slot) in enumerate(pieces):
            start = pl.multiple_of(slot * depth, depth)
            for part in range(2):
                action(
                    pltpu.make_async_copy(
                        source.at[part],
                        factors.at[:, pl.ds(start, depth), pl.ds(part * width, width)],
                        factor_sems.at[number, part],
                    )
                )

    def each_near(action):
        @pl.loop(0, slices)
        def _(part):
            found = table_ref[supernode, place * slices + part]

            @pl.when(found >= 0)
            def _():
                for half in range(2):
                    action(
                        pltpu.make_async_copy(
                            partner_ref.at[supernode, half, part],
                            factors.at[found, pl.ds(near_start, depth), pl.ds(half * width, width)],
                            near_sems.at[part, half],
                        )
                    )

    def out_copy(part, action):
        panel_rows = pl.ds(pl.multiple_of(part * width, width), width)

        @pl.when(keeps)
        def _():
            action(
                pltpu.make_async_copy(out32.at[part], kept_ref.at[panel_rows, :], out_sems.at[part])
            )

        @pl.when(jnp.logical_not(keeps))
        def _():
            action(
                pltpu.make_async_copy(out16.at[part], sent_ref.at[panel_rows, :], out_sems.at[part])
            )

    @pl.when(place_ref[1] == role)
    def _():
        each_piece(lambda copy: copy.start())
        if role:
            each_near(lambda copy: copy.start())
        else:
            before = pltpu.make_async_copy(diag_in_ref.at[supernode], total, diag_sem)
            before.start()

        @pl.loop(0, slices)
        def _(part):
            @pl.when(table_ref[supernode, place * slices + part] >= 0)
            def _():
                @pl.loop(0, listed_count)
                def _(item):
                    column = pl.multiple_of(listed_ref[supernode, item] * width, width)
                    start = pl.multiple_of(part * width, width)
                    pltpu.make_async_copy(
                        pool_ref.at[0, :, pl.ds(start, width), pl.ds(column, width)],
                        rows.at[part, :, :, pl.ds(pl.multiple_of(item * width, width), width)],
                        row_sems.at[part],
                    ).start()

        if columns_ref is not None:
            lent_copy = pltpu.make_async_copy(columns_ref.at[lent_item], columns, column_sem)
            lent_copy.start()
        if role:

            @pl.loop(0, listed_count)
            def _(item):
                block = listed_ref[supernode, item]

                @pl.when(jnp.logical_or(block < end_block, block >= end_block + slices))
                def _():
                    factors[item, pl.ds(near_start, depth), :] = jnp.zeros(
                        (depth, 2 * width), factors.dtype
                    )

            total[...] = jnp.zeros(total.shape, total.dtype)
        else:
            before.wait()

        weight_real = weight_ref[0, 0]
        weight_imag = weight_ref[0, 1]

        @pl.when(place == supernode)
        def _():
            total[...] += weight_real * local_ref[0, 1].astype(jnp.float32) + weight_imag * local_ref[
                0, 0
            ].astype(jnp.float32)

        def add_diagonal(found, both):
            crossed = turned_product(factors[found], both)
            diag_real = -(crossed[:width, :width] - crossed[width:, width:])
            diag_imag = -(crossed[:width, width:] + crossed[width:, :width])
            total[...] += weight_real * diag_imag + weight_imag * diag_real

        each_piece(lambda copy: copy.wait())
        if role:
            each_near(lambda copy: copy.wait())

        @pl.loop(0, slices)
        def _(part):
            found = table_ref[supernode, place * slices + part]

            @pl.when(found < 0)
            def _():
                out32[part] = jnp.zeros((width, width), out32.dtype)
                out16[part] = jnp.zeros((width, width), out16.dtype)

            @pl.when(found >= 0)
            def _():
                pltpu.make_async_copy(
                    pool_ref.at[0, :, pl.ds(0, width), pl.ds(0, listed_count * width)],
                    rows.at[part],
                    row_sems.at[part],
                ).wait()
                stacked = factors[...].reshape(listed_count * 4 * depth, 2 * width)
                by_real = plain_product(rows[part, 0], stacked)
                by_imag = plain_product(rows[part, 1], stacked)
                real = -(by_real[:, :width] - by_imag[:, width:])
                imag = -(by_real[:, width:] + by_imag[:, :width])
                panel = weight_real * imag + weight_imag * real
                out32[part] = panel
                out16[part] = panel.astype(out16.dtype)
                add_diagonal(
                    found,
                    jnp.concatenate([real.astype(jnp.bfloat16), imag.astype(jnp.bfloat16)], axis=1),
                )

            out_copy(part, lambda copy: copy.start())

        if columns_ref is not None:
            lent_copy.wait()

            @pl.loop(0, columns.shape[0] // width)
            def _(part):
                found = table_ref[supernode, end_block + part]

                @pl.when(found >= 0)
                def _():
                    start = pl.multiple_of(part * width, width)
                    add_diagonal(found, columns[pl.ds(start, width), :])

        after = pltpu.make_async_copy(total, diag_ref.at[supernode], diag_sem)
        after.start()

        @pl.loop(0, slices)
        def _(part):
            out_copy(part, lambda copy: copy.wait())

        after.wait()


def supernode_terms(
    k, item, role, lent_item, table, listed, places, weights, pool, tiles, parts, local, columns, outputs
):
    width = tiles.shape[5]
    depth = tiles.shape[4]
    listed_count = tiles.shape[3]
    height = pool.shape[2]
    slices = height // width
    fresh = len(outputs) == 1
    first = 10 + len(columns)
    aliases = {first: 2} if fresh else {first + 2: 2, first: 0, first + 1: 1}
    lent_height = columns[0].shape[1] if columns else width
    return pl.pallas_call(
        functools.partial(supernode_kernel, k, item, role, fresh, lent_item),
        out_shape=(
            jax.ShapeDtypeStruct((height, width), jnp.bfloat16),
            jax.ShapeDtypeStruct((height, width), jnp.float32),
            jax.ShapeDtypeStruct((tiles.shape[1], width, width), jnp.float32),
        ),
        in_specs=[SCALARS] * 4
        + [STAYING] * 2
        + [ANYWHERE] * 3
        + [WHOLE]
        + [ANYWHERE] * (len(columns) + len(outputs)),
        out_specs=(ANYWHERE, ANYWHERE, ANYWHERE),
        input_output_aliases=aliases,
        scratch_shapes=[
            pltpu.VMEM((listed_count, 4 * depth, 2 * width), jnp.bfloat16),
            pltpu.VMEM((slices, 2, width, listed_count * width), jnp.bfloat16),
            pltpu.VMEM((slices, width, width), jnp.bfloat16),
            pltpu.VMEM((slices, width, width), jnp.float32),
            pltpu.VMEM((width, width), jnp.float32),
            pltpu.VMEM((lent_height, 2 * width), jnp.bfloat16),
            pltpu.SemaphoreType.DMA((4, 2)),
            pltpu.SemaphoreType.DMA((slices, 2)),
            pltpu.SemaphoreType.DMA((slices,)),
            pltpu.SemaphoreType.DMA((slices,)),
            pltpu.SemaphoreType.DMA,
            pltpu.SemaphoreType.DMA,
        ],
        compiler_params=pltpu.CompilerParams(vmem_limit_bytes=52 * 1024 * 1024),
        cost_estimate=pl.CostEstimate(
            flops=8 * height * width * width * listed_count,
            bytes_accessed=6 * height * width * listed_count,
            transcendentals=0,
        ),
    )(table, listed, places, weights, pool, tiles, *parts, local, *columns, *outputs)


def lent_kernel(
    half,
    known,
    table_ref,
    place_ref,
    weight_ref,
    columns_ref,
    tiles_ref,
    *refs,
):
    part_refs = [refs[3 * c : 3 * c + 3] for c in range(known)]
    refs = refs[3 * known :]
    diag_in_ref = None
    if half:
        diag_in_ref, *refs = refs
    (
        sent_ref,
        kept_ref,
        diag_ref,
        left_ref,
        columns,
        factors,
        matched,
        out16,
        out32,
        total,
        left,
        column_sem,
        factor_sems,
        matched_sems,
        out_sems,
        diag_sem,
        left_sem,
    ) = refs
    supers, width, _ = total.shape
    depth = tiles_ref.shape[4]
    slices = columns.shape[1] // width
    others = factors.shape[1] // depth
    place = place_ref[0]
    edge = place_ref[1]
    first_half = place_ref[2]
    end_block = place_ref[3]
    other_first = place_ref[4]
    chip = place_ref[5]
    weight_real = weight_ref[0, 0]
    weight_imag = weight_ref[0, 1]
    first_block = end_block + half * slices
    ready = [k for group in CHUNKS[:known] for k in group]
    pending = [k for k in range(supers) if k not in ready]

    @pl.when(edge == 0)
    def _():
        whole = pltpu.make_async_copy(columns_ref, columns, column_sem)
        whole.start()
        if half:
            before = pltpu.make_async_copy(diag_in_ref, total, diag_sem)
            before.start()

        @pl.loop(0, supers)
        def _(k):
            @pl.loop(0, others)
            def _(other):
                found = table_ref[k, other_first + other]
                span = pl.ds(pl.multiple_of(other * depth, depth), depth)

                @pl.when(found >= 0)
                def _():
                    for part in range(2):
                        pltpu.make_async_copy(
                            tiles_ref.at[0, k, part, found],
                            factors.at[k, span, pl.ds(part * width, width)],
                            factor_sems.at[k, other],
                        ).start()

                @pl.when(found < 0)
                def _():
                    factors[k, span, :] = jnp.zeros((depth, 2 * width), factors.dtype)

        for chunk, group in enumerate(CHUNKS[:known]):
            swap_ref, near_ref, far_ref = part_refs[chunk]
            for item, k in enumerate(group):

                @pl.loop(0, slices)
                def _(part, k=k, item=item, swap_ref=swap_ref, near_ref=near_ref, far_ref=far_ref):
                    found = table_ref[k, first_block + part]

                    @pl.when(found >= 0)
                    def _():
                        for source, slot in (
                            (tiles_ref.at[0, k], place),
                            (swap_ref.at[item], 3 * (1 - first_half)),
                            (near_ref.at[item], 1 + first_half),
                            (far_ref.at[item], 3 * first_half),
                        ):
                            start = pl.multiple_of(slot * depth, depth)
                            pltpu.make_async_copy(
                                source.at[:, found],
                                matched.at[k, part, :, pl.ds(start, depth), :],
                                matched_sems.at[k, part],
                            ).start()

        if half:
            before.wait()
        else:
            total[...] = jnp.zeros(total.shape, total.dtype)
        whole.wait()

        def out_copy(k, part, action):
            panel_rows = pl.ds(pl.multiple_of(part * width, width), width)
            slot = lax.rem(k, 2)

            @pl.when(chip == k // 2)
            def _():
                action(
                    pltpu.make_async_copy(
                        out32.at[slot, part], kept_ref.at[slot, panel_rows, :], out_sems.at[k, part]
                    )
                )

            @pl.when(chip != k // 2)
            def _():
                action(
                    pltpu.make_async_copy(
                        out16.at[slot, part], sent_ref.at[slot, panel_rows, :], out_sems.at[k, part]
                    )
                )

        @pl.loop(0, supers)
        def _(k):
            @pl.loop(0, others)
            def _(other):
                span = pl.ds(pl.multiple_of(other * depth, depth), depth)

                @pl.when(table_ref[k, other_first + other] >= 0)
                def _():
                    pltpu.make_async_copy(
                        factors.at[k, span, :], factors.at[k, span, :], factor_sems.at[k, other]
                    ).wait()

            slot = lax.rem(k, 2)
            mine = chip == k // 2

            @pl.loop(0, slices)
            def _(part):
                found = table_ref[k, first_block + part]
                panel_rows = pl.ds(pl.multiple_of(part * width, width), width)

                def store(panel):
                    @pl.when(mine)
                    def _():
                        out32[slot, part] = panel

                    @pl.when(jnp.logical_not(mine))
                    def _():
                        out16[slot, part] = panel.astype(out16.dtype)

                @pl.when(found < 0)
                def _():
                    store(jnp.zeros((width, width), jnp.float32))

                @pl.when(found >= 0)
                def _():
                    by_real = plain_product(columns[0, panel_rows, :], factors[k])
                    by_imag = plain_product(columns[1, panel_rows, :], factors[k])
                    real = -(by_real[:, :width] - by_imag[:, width:])
                    imag = -(by_real[:, width:] + by_imag[:, :width])
                    store(weight_real * imag + weight_imag * real)
                    both = jnp.concatenate(
                        [real.astype(jnp.bfloat16), imag.astype(jnp.bfloat16)], axis=1
                    )

                    def with_diagonal():
                        pltpu.make_async_copy(
                            matched.at[k, part], matched.at[k, part], matched_sems.at[k, part]
                        ).wait()
                        crossed_real = turned_product(matched[k, part, 0], both)
                        crossed_imag = turned_product(matched[k, part, 1], both)
                        diag_real = -(crossed_real[:, :width] - crossed_imag[:, width:])
                        diag_imag = -(crossed_real[:, width:] + crossed_imag[:, :width])
                        total[k] += weight_real * diag_imag + weight_imag * diag_real

                    if pending:
                        is_pending = functools.reduce(jnp.logical_or, [k == p for p in pending])
                        pl.when(jnp.logical_not(is_pending))(with_diagonal)
                        place_in = sum(
                            jnp.where(k == p, index, 0) for index, p in enumerate(pending)
                        )

                        @pl.when(is_pending)
                        def _():
                            left[place_in, panel_rows, :] = both
                    else:
                        with_diagonal()

                out_copy(k, part, lambda copy: copy.start())

        after = pltpu.make_async_copy(total, diag_ref, diag_sem)
        after.start()
        if pending:
            keep = pltpu.make_async_copy(left, left_ref, left_sem)
            keep.start()
            keep.wait()

        @pl.loop(0, supers)
        def _(k):
            @pl.loop(0, slices)
            def _(part):
                out_copy(k, part, lambda copy: copy.wait())

        after.wait()


def lent_terms(half, known, table, places, weights, columns, tiles, parts, outputs):
    supers = tiles.shape[1]
    width = tiles.shape[5]
    depth = tiles.shape[4]
    height = columns.shape[1]
    slices = height // width
    others = columns.shape[2] // depth
    left = max(1, supers - sum(len(group) for group in CHUNKS[:known]))
    left_shape = (left, height, 2 * width)
    return pl.pallas_call(
        functools.partial(lent_kernel, half, known),
        out_shape=(
            jax.ShapeDtypeStruct((2, height, width), jnp.bfloat16),
            jax.ShapeDtypeStruct((2, height, width), jnp.float32),
            jax.ShapeDtypeStruct((supers, width, width), jnp.float32),
            jax.ShapeDtypeStruct(left_shape, jnp.bfloat16),
        ),
        in_specs=[SCALARS] * 3 + [ANYWHERE] * (2 + 3 * known + len(outputs)),
        out_specs=(ANYWHERE,) * 4,
        input_output_aliases={5 + 3 * known: 2} if outputs else {},
        scratch_shapes=[
            pltpu.VMEM(columns.shape, columns.dtype),
            pltpu.VMEM((supers, others * depth, 2 * width), tiles.dtype),
            pltpu.VMEM((supers, slices, 2, 4 * depth, width), tiles.dtype),
            pltpu.VMEM((2, slices, width, width), jnp.bfloat16),
            pltpu.VMEM((2, slices, width, width), jnp.float32),
            pltpu.VMEM((supers, width, width), jnp.float32),
            pltpu.VMEM(left_shape, jnp.bfloat16),
            pltpu.SemaphoreType.DMA,
            pltpu.SemaphoreType.DMA((supers, others)),
            pltpu.SemaphoreType.DMA((supers, slices)),
            pltpu.SemaphoreType.DMA((supers, slices)),
            pltpu.SemaphoreType.DMA,
            pltpu.SemaphoreType.DMA,
        ],
        compiler_params=pltpu.CompilerParams(vmem_limit_bytes=52 * 1024 * 1024),
        cost_estimate=pl.CostEstimate(
            flops=8 * height * supers * width * others * depth,
            bytes_accessed=8 * supers * others * depth * width,
            transcendentals=0,
        ),
    )(table, places, weights, columns, tiles, *parts, *outputs)


def shards_line(inverse_pool, factor_tiles, diag_inverse, pole_weight, ancestors):
    supers = factor_tiles.shape[1]
    listed_count = factor_tiles.shape[3]
    depth = factor_tiles.shape[4]
    width = factor_tiles.shape[5]
    height = inverse_pool.shape[2]
    slices = height // width
    blocks = inverse_pool.shape[3] // width
    place = lax.axis_index("grid")
    pole = lax.axis_index("pole")
    chip = pole // 2
    core = pole % 2
    edge = jnp.logical_or(place == 0, place == 3)
    first_half = (place < 2).astype(jnp.int32)
    places = jnp.stack(
        [place, edge.astype(jnp.int32), first_half, 3 * slices * (1 - first_half), slices * first_half, chip]
    ).astype(jnp.int32)
    same = ancestors[:, :, None] == jnp.arange(blocks, dtype=jnp.int32)
    table = jnp.max(
        jnp.where(same, jnp.arange(listed_count, dtype=jnp.int32)[None, :, None], -1), axis=1
    ).astype(jnp.int32)

    def planes(places_z, pairs):
        return [(4 * z + a, 4 * z + b) for z in places_z for a, b in pairs]

    def halves(value, which, axis):
        size = value.shape[axis] // 2
        return (
            lax.dynamic_slice_in_dim(value, (1 - which) * size, size, axis),
            lax.dynamic_slice_in_dim(value, which * size, size, axis),
        )

    def joined(mine, other, which):
        return jnp.where(which == 0, jnp.concatenate([mine, other]), jnp.concatenate([other, mine]))

    owns = [jnp.stack([factor_tiles[0, k] for k in group]) for group in CHUNKS]
    near_rows = pl.pallas_call(
        near_rows_kernel,
        out_shape=jax.ShapeDtypeStruct((supers, 2, slices, depth, width), factor_tiles.dtype),
        in_specs=[SCALARS] * 2 + [ANYWHERE],
        out_specs=WHOLE,
        scratch_shapes=[pltpu.SemaphoreType.DMA((supers, slices))],
        name="near_rows",
    )(table, places, factor_tiles)
    near = lax.ppermute(near_rows, "grid", OUTWARD_Z)
    lent = []
    for half in range(2):
        packed = packed_columns(places, inverse_pool, depth, width, half, 2)
        lent.append(lax.ppermute(packed, "grid", INWARD_Z))

    parts = []
    for own in owns:
        swap = lax.ppermute(own, "grid", INWARD_Z)
        mid_near = lax.ppermute(own, "grid", MIDDLE_Z)
        mid_far = lax.ppermute(swap, "grid", MIDDLE_Z)
        end_near = lax.ppermute(mid_near, "grid", OUTWARD_Z)
        end_far = lax.ppermute(mid_far, "grid", OUTWARD_Z)
        parts.append((swap, mid_near, mid_far, end_near, end_far))

    both_axes = ("grid", "pole")
    middles = [piece for part in parts for piece in part[:3]]
    common = (table, ancestors, places, pole_weight, inverse_pool, factor_tiles)

    def node(k, role, columns, outputs):
        c = next(c for c, group in enumerate(CHUNKS) if k in group)
        swap, mid_near, mid_far, end_near, end_far = parts[c]
        wanted = (near, end_near, end_far) if role else (swap, mid_near, mid_far)
        return supernode_terms(
            k, CHUNKS[c].index(k), role, k - 1 if columns else None, *common, wanted,
            diag_inverse, columns, outputs,
        )

    def lent_node(half, known, outputs):
        return lent_terms(
            half, known, table, places, pole_weight, lent[half], factor_tiles,
            middles[: 3 * known], outputs,
        )

    lent_sent, lent_kept = [None] * 2, [None] * 2
    lent_sent[0], lent_kept[0], diag, columns = lent_node(0, 1, ())
    outer = node(0, 0, (), (diag,))
    outer = node(3, 0, (), outer)
    outer = node(0, 1, (), outer)
    sent_outer, kept_outer, diag = node(3, 1, (), outer)
    inner = node(1, 0, (columns,), (diag,))
    inner = node(2, 0, (columns,), inner)
    lent_sent[1], lent_kept[1], diag, _ = lent_node(1, len(CHUNKS), (inner[2],))
    sent_inner, kept_inner, diag = node(1, 1, (), (inner[0], inner[1], diag))
    sent_inner, kept_inner, diag = node(2, 1, (), (sent_inner, kept_inner, diag))

    returned = []
    for half in range(2):
        both = lent_kept[half] + lax.ppermute(
            lent_sent[half], both_axes, planes((1, 2), ACROSS_X)
        ).astype(jnp.float32)
        mine = jnp.where(core == 0, both[0], both[1])
        yours = jnp.where(core == 0, both[1], both[0])
        mine = mine + lax.ppermute(yours, both_axes, planes((1, 2), PAIRS_Z))
        returned.append(lax.ppermute(mine.astype(jnp.bfloat16), "grid", OUTWARD_Z))

    chip_sum = kept_outer + lax.ppermute(sent_outer, "pole", ACROSS_X).astype(jnp.float32)
    base = chip_sum + lax.ppermute(chip_sum, "pole", [(1, 0), (2, 3)])
    in_outer = jnp.logical_or(pole == 0, pole == 3)
    back = jnp.concatenate(returned).astype(jnp.float32)
    base = jnp.where(in_outer, base, 0.0) + jnp.where(edge, back, 0.0)
    base = lax.optimization_barrier(base)
    chip_sum = kept_inner + lax.ppermute(sent_inner, "pole", ACROSS_X).astype(jnp.float32)
    last = chip_sum + lax.ppermute(chip_sum, "pole", [(0, 1), (3, 2)])
    panel_share = base + jnp.where(in_outer, 0.0, last)

    def to_quarters(value, places_z):
        sent, kept = halves(value, core, 1)
        value = kept + lax.ppermute(sent, both_axes, planes(places_z, PAIRS_Z))
        sent, kept = halves(value, chip, 1)
        return kept + lax.ppermute(sent, both_axes, planes(places_z, ACROSS_X))

    quarters = to_quarters(diag, range(4))
    own = lax.dynamic_index_in_dim(quarters, place, 0, keepdims=False)
    for shift in range(1, 4):
        sent = lax.dynamic_index_in_dim(quarters, (place + shift) % 4, 0, keepdims=False)
        own = own + lax.ppermute(sent, "grid", [(z, (z + shift) % 4) for z in range(4)])
    own = joined(own, lax.ppermute(own, "pole", ACROSS_X), chip)
    diag_share = joined(own, lax.ppermute(own, "pole", PAIRS_Z), core)
    return (panel_share, diag_share)


def solution(mesh):
    in_specs = (
        P(("ens", "pole"), None, "grid", None),
        P(("ens", "pole"), None, None, None, "grid", None),
        P(("ens", "pole"), None, "grid", None),
        P("pole", None),
        P(),
    )
    out_specs = (P(("ens", "grid"), "pole"), P(("ens", "grid"), None))

    def shards(inverse_pool, factor_tiles, diag_inverse, pole_weight, ancestors):
        groups = mesh.shape["grid"]
        poles = mesh.shape["pole"]
        supers = factor_tiles.shape[1]
        width = factor_tiles.shape[5]
        line = (
            groups == 4
            and poles == 4
            and supers == 4
            and factor_tiles.shape[4] * groups == width
            and inverse_pool.shape[2] % width == 0
            and diag_inverse.shape[2] == width
            and width % 256 == 0
        )
        if not line:
            return shards_any(inverse_pool, factor_tiles, diag_inverse, pole_weight, ancestors)
        return shards_line(inverse_pool, factor_tiles, diag_inverse, pole_weight, ancestors)

    return jax.shard_map(shards, mesh=mesh, in_specs=in_specs, out_specs=out_specs, check_vma=False)
```

```python
import functools

import jax
import jax.numpy as jnp
from jax import lax
from jax.experimental import pallas as pl
from jax.experimental.pallas import tpu as pltpu
from jax.sharding import PartitionSpec as P


def plain_product(left, right):
    return jnp.dot(left, right, preferred_element_type=jnp.float32)


def turned_product(left, right):
    return lax.dot_general(
        left, right, (((0,), (0,)), ((), ())), preferred_element_type=jnp.float32
    )


def portion_terms(rows_pair, block_index, offset, listed, factors, weights):
    tile_width = factors.shape[3]
    listed_count = factors.shape[1]
    height = rows_pair.shape[1]
    blocks = rows_pair.shape[2] // tile_width
    matches = listed == block_index

    def compute():
        chosen = rows_pair.reshape(2, height, blocks, tile_width)[:, :, listed, :].reshape(
            2, height, listed_count * tile_width
        )
        stacked = factors.reshape(2, listed_count * tile_width, tile_width)
        part_real = -(plain_product(chosen[0], stacked[0]) - plain_product(chosen[1], stacked[1]))
        part_imag = -(plain_product(chosen[0], stacked[1]) + plain_product(chosen[1], stacked[0]))
        panel_piece = weights[0] * part_imag + weights[1] * part_real
        rounded_real = part_real.astype(jnp.bfloat16)
        rounded_imag = part_imag.astype(jnp.bfloat16)
        position = jnp.sum(jnp.where(matches, jnp.arange(listed_count, dtype=jnp.int32), 0))
        matched = lax.dynamic_slice(
            factors, (jnp.int32(0), position, offset, jnp.int32(0)), (2, 1, height, tile_width)
        )[:, 0]
        diag_real = -(
            turned_product(matched[0], rounded_real) - turned_product(matched[1], rounded_imag)
        )
        diag_imag = -(
            turned_product(matched[0], rounded_imag) + turned_product(matched[1], rounded_real)
        )
        return (panel_piece, weights[0] * diag_imag + weights[1] * diag_real)

    def skipped():
        return (
            jnp.zeros((height, tile_width), jnp.float32),
            jnp.zeros((tile_width, tile_width), jnp.float32),
        )

    return lax.cond(jnp.any(matches), compute, skipped)


def rows_terms(rows_pair, row_first, listed, factors, weights):
    tile_width = factors.shape[3]
    height = rows_pair.shape[1]
    piece_rows = min(height, tile_width)
    panels = []
    diag_total = jnp.zeros((tile_width, tile_width), jnp.float32)
    for portion in range(height // piece_rows):
        row_start = row_first + portion * piece_rows
        panel_piece, diag_piece = portion_terms(
            rows_pair[:, portion * piece_rows : (portion + 1) * piece_rows],
            row_start // tile_width,
            row_start % tile_width,
            listed,
            factors,
            weights,
        )
        panels.append(panel_piece)
        diag_total = diag_total + diag_piece
    return (jnp.concatenate(panels, axis=0), diag_total)


def shards_any(inverse_pool, factor_tiles, diag_inverse, pole_weight, ancestors):
    device_index = lax.axis_index("grid")
    rows_here = inverse_pool.shape[2]
    supers = factor_tiles.shape[1]
    tile_width = factor_tiles.shape[5]
    row_slab = inverse_pool[0]
    weights = (pole_weight[0, 0], pole_weight[0, 1])
    row_first = device_index * rows_here
    own_panels = []
    diag_terms = []
    for supernode in range(supers):
        factors = lax.all_gather(factor_tiles[0, supernode], "grid", axis=2, tiled=True)
        listed = ancestors[supernode]
        own_panel, own_diag = rows_terms(row_slab, row_first, listed, factors, weights)
        diag_terms.append(own_diag)
        own_panels.append(own_panel)
    panel_rows = jnp.concatenate(own_panels, axis=1)
    panel_share = lax.psum_scatter(panel_rows, "pole", scatter_dimension=1, tiled=True)
    diag_term = jnp.stack(diag_terms, axis=0).reshape(supers * tile_width, tile_width)
    diag_local = diag_inverse[0]
    local_block = weights[0] * diag_local[1].astype(jnp.float32) + weights[1] * diag_local[
        0
    ].astype(jnp.float32)
    share_rows = local_block.shape[0]
    placed = lax.dynamic_update_slice(
        jnp.zeros_like(diag_term), local_block, (device_index * share_rows, jnp.int32(0))
    )
    spread = lax.psum_scatter(diag_term + placed, ("grid", "pole"), scatter_dimension=0, tiled=True)
    diag_share = lax.all_gather(spread, "pole", axis=0, tiled=True)
    return (panel_share, diag_share)


PAIRS_Z = [(0, 1), (1, 0), (2, 3), (3, 2)]
MIDDLE_Z = [(1, 2), (2, 1)]
OUTWARD_Z = [(1, 0), (2, 3)]
INWARD_Z = [(0, 1), (3, 2)]
ACROSS_X = [(0, 2), (2, 0), (1, 3), (3, 1)]
CHUNKS = ((0, 3), (1,), (2,))


ANYWHERE = pl.BlockSpec(memory_space=pl.ANY)
STAYING = pl.BlockSpec(memory_space=pltpu.MemorySpace.HBM)
SCALARS = pl.BlockSpec(memory_space=pltpu.SMEM)
WHOLE = pl.BlockSpec(memory_space=pltpu.VMEM)


def near_rows_kernel(table_ref, place_ref, tiles_ref, out_ref, sems):
    supers = out_ref.shape[0]
    slices = out_ref.shape[2]
    end_block = place_ref[3]

    def each(action):
        for k in range(supers):
            for part in range(slices):
                found = table_ref[k, end_block + part]

                @pl.when(found >= 0)
                def _(k=k, part=part, found=found):
                    action(
                        pltpu.make_async_copy(
                            tiles_ref.at[0, k, :, found],
                            out_ref.at[k, :, part],
                            sems.at[k, part],
                        )
                    )

    each(lambda copy: copy.start())
    each(lambda copy: copy.wait())


def pack_columns_kernel(depth, width, place_ref, pool_ref, out_ref):
    first_half = place_ref[2]
    blocks = pool_ref.shape[3] // width

    @pl.when(place_ref[1] == 1)
    def _():
        for offset, flag in ((depth, 1), (2 * depth, 0)):

            @pl.when(first_half == flag)
            def _(offset=offset):
                for part in range(2):
                    out_ref[part] = jnp.concatenate(
                        [
                            pool_ref[0, part, :, q * width + offset : q * width + offset + depth]
                            for q in range(blocks)
                        ],
                        axis=1,
                    )


def packed_columns(places, pool, depth, width, half, halves):
    height = pool.shape[2] // halves
    slices = pool.shape[2] // width
    tile = min(height, width)
    steps = height // tile
    groups = pool.shape[3] // (slices * width) - 1
    return pl.pallas_call(
        functools.partial(pack_columns_kernel, depth, width),
        out_shape=jax.ShapeDtypeStruct((2, height, groups * slices * depth), pool.dtype),
        grid_spec=pltpu.PrefetchScalarGridSpec(
            num_scalar_prefetch=1,
            grid=(steps, groups),
            in_specs=[
                pl.BlockSpec(
                    (1, 2, tile, slices * width),
                    lambda i, j, place: (0, 0, (half * steps + i) * place[1], (j + place[2]) * place[1]),
                )
            ],
            out_specs=pl.BlockSpec(
                (2, tile, slices * depth), lambda i, j, place: (0, i * place[1], j * place[1])
            ),
        ),
        cost_estimate=pl.CostEstimate(
            flops=0, bytes_accessed=3 * pool.shape[3] * height * 2, transcendentals=0
        ),
    )(places, pool)


def supernode_kernel(
    supernode,
    item_in_chunk,
    role,
    fresh,
    lent_item,
    table_ref,
    listed_ref,
    place_ref,
    weight_ref,
    pool_ref,
    tiles_ref,
    partner_ref,
    far_near_ref,
    far_far_ref,
    local_ref,
    *refs,
):
    columns_ref = None
    if lent_item is not None:
        columns_ref, *refs = refs
    diag_in_ref = refs[0] if fresh else refs[2]
    refs = refs[1:] if fresh else refs[3:]
    (
        sent_ref,
        kept_ref,
        diag_ref,
        factors,
        rows,
        out16,
        out32,
        total,
        columns,
        factor_sems,
        near_sems,
        row_sems,
        out_sems,
        diag_sem,
        column_sem,
    ) = refs
    width = total.shape[0]
    listed_count = factors.shape[0]
    slices = rows.shape[0]
    depth = tiles_ref.shape[4]
    place = place_ref[0]
    first_half = place_ref[2]
    end_block = place_ref[3]
    keeps = place_ref[5] == supernode // 2
    odd = lax.rem(place, 2)

    own_base = 2 * (1 - first_half)
    far_base = 2 * first_half
    near_slot = 1 - first_half
    near_start = pl.multiple_of((1 - odd + own_base) * depth, depth)
    pieces = [
        (tiles_ref.at[0, supernode], odd + own_base),
        (far_near_ref.at[item_in_chunk], near_slot + far_base),
        (far_far_ref.at[item_in_chunk], 1 - near_slot + far_base),
    ]
    if not role:
        pieces.append((partner_ref.at[item_in_chunk], 1 - odd + own_base))

    def each_piece(action):
        for number, (source, slot) in enumerate(pieces):
            start = pl.multiple_of(slot * depth, depth)
            for part in range(2):
                action(
                    pltpu.make_async_copy(
                        source.at[part],
                        factors.at[:, pl.ds(start, depth), pl.ds(part * width, width)],
                        factor_sems.at[number, part],
                    )
                )

    def each_near(action):
        @pl.loop(0, slices)
        def _(part):
            found = table_ref[supernode, place * slices + part]

            @pl.when(found >= 0)
            def _():
                for half in range(2):
                    action(
                        pltpu.make_async_copy(
                            partner_ref.at[supernode, half, part],
                            factors.at[found, pl.ds(near_start, depth), pl.ds(half * width, width)],
                            near_sems.at[part, half],
                        )
                    )

    def store(part, panel):
        @pl.when(keeps)
        def _():
            out32[part] = panel

        @pl.when(jnp.logical_not(keeps))
        def _():
            out16[part] = panel.astype(out16.dtype)

    def out_copy(part, action):
        panel_rows = pl.ds(pl.multiple_of(part * width, width), width)

        @pl.when(keeps)
        def _():
            action(
                pltpu.make_async_copy(out32.at[part], kept_ref.at[panel_rows, :], out_sems.at[part])
            )

        @pl.when(jnp.logical_not(keeps))
        def _():
            action(
                pltpu.make_async_copy(out16.at[part], sent_ref.at[panel_rows, :], out_sems.at[part])
            )

    @pl.when(place_ref[1] == role)
    def _():
        each_piece(lambda copy: copy.start())
        if role:
            each_near(lambda copy: copy.start())
        else:
            before = pltpu.make_async_copy(diag_in_ref.at[supernode], total, diag_sem)
            before.start()

        @pl.loop(0, slices)
        def _(part):
            @pl.when(table_ref[supernode, place * slices + part] >= 0)
            def _():
                @pl.loop(0, listed_count)
                def _(item):
                    column = pl.multiple_of(listed_ref[supernode, item] * width, width)
                    start = pl.multiple_of(part * width, width)
                    pltpu.make_async_copy(
                        pool_ref.at[0, :, pl.ds(start, width), pl.ds(column, width)],
                        rows.at[part, :, :, pl.ds(pl.multiple_of(item * width, width), width)],
                        row_sems.at[part],
                    ).start()

        if columns_ref is not None:
            lent_copy = pltpu.make_async_copy(columns_ref.at[lent_item], columns, column_sem)
            lent_copy.start()
        if role:

            @pl.loop(0, listed_count)
            def _(item):
                block = listed_ref[supernode, item]

                @pl.when(jnp.logical_or(block < end_block, block >= end_block + slices))
                def _():
                    factors[item, pl.ds(near_start, depth), :] = jnp.zeros(
                        (depth, 2 * width), factors.dtype
                    )

            total[...] = jnp.zeros(total.shape, total.dtype)
        else:
            before.wait()

        weight_real = weight_ref[0, 0]
        weight_imag = weight_ref[0, 1]

        @pl.when(place == supernode)
        def _():
            total[...] += weight_real * local_ref[0, 1].astype(jnp.float32) + weight_imag * local_ref[
                0, 0
            ].astype(jnp.float32)

        def add_diagonal(found, both):
            crossed = turned_product(factors[found], both)
            diag_real = -(crossed[:width, :width] - crossed[width:, width:])
            diag_imag = -(crossed[:width, width:] + crossed[width:, :width])
            total[...] += weight_real * diag_imag + weight_imag * diag_real

        each_piece(lambda copy: copy.wait())
        if role:
            each_near(lambda copy: copy.wait())

        @pl.loop(0, slices)
        def _(part):
            found = table_ref[supernode, place * slices + part]

            @pl.when(found < 0)
            def _():
                store(part, jnp.zeros((width, width), jnp.float32))

            @pl.when(found >= 0)
            def _():
                pltpu.make_async_copy(
                    pool_ref.at[0, :, pl.ds(0, width), pl.ds(0, listed_count * width)],
                    rows.at[part],
                    row_sems.at[part],
                ).wait()
                stacked = factors[...].reshape(listed_count * 4 * depth, 2 * width)
                by_real = plain_product(rows[part, 0], stacked)
                by_imag = plain_product(rows[part, 1], stacked)
                real = -(by_real[:, :width] - by_imag[:, width:])
                imag = -(by_real[:, width:] + by_imag[:, :width])
                store(part, weight_real * imag + weight_imag * real)
                add_diagonal(
                    found,
                    jnp.concatenate([real.astype(jnp.bfloat16), imag.astype(jnp.bfloat16)], axis=1),
                )

            out_copy(part, lambda copy: copy.start())

        if columns_ref is not None:
            lent_copy.wait()

            @pl.loop(0, columns.shape[0] // width)
            def _(part):
                found = table_ref[supernode, end_block + part]

                @pl.when(found >= 0)
                def _():
                    start = pl.multiple_of(part * width, width)
                    add_diagonal(found, columns[pl.ds(start, width), :])

        after = pltpu.make_async_copy(total, diag_ref.at[supernode], diag_sem)
        after.start()

        @pl.loop(0, slices)
        def _(part):
            out_copy(part, lambda copy: copy.wait())

        after.wait()


def supernode_terms(
    k, item, role, lent_item, table, listed, places, weights, pool, tiles, parts, local, columns, outputs
):
    width = tiles.shape[5]
    depth = tiles.shape[4]
    listed_count = tiles.shape[3]
    height = pool.shape[2]
    slices = height // width
    fresh = len(outputs) == 1
    first = 10 + len(columns)
    aliases = {first: 2} if fresh else {first + 2: 2, first: 0, first + 1: 1}
    lent_height = columns[0].shape[1] if columns else width
    return pl.pallas_call(
        functools.partial(supernode_kernel, k, item, role, fresh, lent_item),
        out_shape=(
            jax.ShapeDtypeStruct((height, width), jnp.bfloat16),
            jax.ShapeDtypeStruct((height, width), jnp.float32),
            jax.ShapeDtypeStruct((tiles.shape[1], width, width), jnp.float32),
        ),
        in_specs=[SCALARS] * 4
        + [STAYING] * 2
        + [ANYWHERE] * 3
        + [WHOLE]
        + [ANYWHERE] * (len(columns) + len(outputs)),
        out_specs=(ANYWHERE, ANYWHERE, ANYWHERE),
        input_output_aliases=aliases,
        scratch_shapes=[
            pltpu.VMEM((listed_count, 4 * depth, 2 * width), jnp.bfloat16),
            pltpu.VMEM((slices, 2, width, listed_count * width), jnp.bfloat16),
            pltpu.VMEM((slices, width, width), jnp.bfloat16),
            pltpu.VMEM((slices, width, width), jnp.float32),
            pltpu.VMEM((width, width), jnp.float32),
            pltpu.VMEM((lent_height, 2 * width), jnp.bfloat16),
            pltpu.SemaphoreType.DMA((4, 2)),
            pltpu.SemaphoreType.DMA((slices, 2)),
            pltpu.SemaphoreType.DMA((slices,)),
            pltpu.SemaphoreType.DMA((slices,)),
            pltpu.SemaphoreType.DMA,
            pltpu.SemaphoreType.DMA,
        ],
        compiler_params=pltpu.CompilerParams(vmem_limit_bytes=48 * 1024 * 1024),
        cost_estimate=pl.CostEstimate(
            flops=8 * height * width * width * listed_count,
            bytes_accessed=6 * height * width * listed_count,
            transcendentals=0,
        ),
    )(table, listed, places, weights, pool, tiles, *parts, local, *columns, *outputs)


def lent_kernel(
    half,
    known,
    table_ref,
    place_ref,
    weight_ref,
    columns_ref,
    tiles_ref,
    *refs,
):
    part_refs = [refs[3 * c : 3 * c + 3] for c in range(known)]
    refs = refs[3 * known :]
    diag_in_ref = None
    if half:
        diag_in_ref, *refs = refs
    (
        sent_ref,
        kept_ref,
        diag_ref,
        left_ref,
        columns,
        factors,
        matched,
        out16,
        out32,
        total,
        left,
        column_sem,
        factor_sems,
        matched_sems,
        out_sems,
        diag_sem,
        left_sem,
    ) = refs
    supers, width, _ = total.shape
    depth = tiles_ref.shape[4]
    slices = columns.shape[1] // width
    others = factors.shape[2] // depth
    place = place_ref[0]
    edge = place_ref[1]
    first_half = place_ref[2]
    end_block = place_ref[3]
    other_first = place_ref[4]
    chip = place_ref[5]
    weight_real = weight_ref[0, 0]
    weight_imag = weight_ref[0, 1]
    first_block = end_block + half * slices
    ready = [k for group in CHUNKS[:known] for k in group]
    pending = [k for k in range(supers) if k not in ready]

    @pl.when(edge == 0)
    def _():
        whole = pltpu.make_async_copy(columns_ref, columns, column_sem)
        whole.start()
        if half:
            before = pltpu.make_async_copy(diag_in_ref, total, diag_sem)
            before.start()

        @pl.loop(0, supers)
        def _(k):
            @pl.loop(0, others)
            def _(other):
                found = table_ref[k, other_first + other]
                span = pl.ds(pl.multiple_of(other * depth, depth), depth)

                @pl.when(found >= 0)
                def _():
                    pltpu.make_async_copy(
                        tiles_ref.at[0, k, :, found],
                        factors.at[k, :, span, :],
                        factor_sems.at[k, other],
                    ).start()

                @pl.when(found < 0)
                def _():
                    factors[k, :, span, :] = jnp.zeros((2, depth, width), factors.dtype)

        for chunk, group in enumerate(CHUNKS[:known]):
            swap_ref, near_ref, far_ref = part_refs[chunk]
            for item, k in enumerate(group):

                @pl.loop(0, slices)
                def _(part, k=k, item=item, swap_ref=swap_ref, near_ref=near_ref, far_ref=far_ref):
                    found = table_ref[k, first_block + part]

                    @pl.when(found >= 0)
                    def _():
                        for source, slot in (
                            (tiles_ref.at[0, k], place),
                            (swap_ref.at[item], 3 * (1 - first_half)),
                            (near_ref.at[item], 1 + first_half),
                            (far_ref.at[item], 3 * first_half),
                        ):
                            start = pl.multiple_of(slot * depth, depth)
                            pltpu.make_async_copy(
                                source.at[:, found],
                                matched.at[k, part, :, pl.ds(start, depth), :],
                                matched_sems.at[k, part],
                            ).start()

        if half:
            before.wait()
        else:
            total[...] = jnp.zeros(total.shape, total.dtype)
        whole.wait()

        def out_copy(k, part, action):
            panel_rows = pl.ds(pl.multiple_of(part * width, width), width)
            slot = lax.rem(k, 2)

            @pl.when(chip == k // 2)
            def _():
                action(
                    pltpu.make_async_copy(
                        out32.at[slot, part], kept_ref.at[slot, panel_rows, :], out_sems.at[k, part]
                    )
                )

            @pl.when(chip != k // 2)
            def _():
                action(
                    pltpu.make_async_copy(
                        out16.at[slot, part], sent_ref.at[slot, panel_rows, :], out_sems.at[k, part]
                    )
                )

        @pl.loop(0, supers)
        def _(k):
            @pl.loop(0, others)
            def _(other):
                span = pl.ds(pl.multiple_of(other * depth, depth), depth)

                @pl.when(table_ref[k, other_first + other] >= 0)
                def _():
                    pltpu.make_async_copy(
                        factors.at[k, :, span, :], factors.at[k, :, span, :], factor_sems.at[k, other]
                    ).wait()

            slot = lax.rem(k, 2)
            mine = chip == k // 2

            @pl.loop(0, slices)
            def _(part):
                found = table_ref[k, first_block + part]
                panel_rows = pl.ds(pl.multiple_of(part * width, width), width)

                def store(panel):
                    @pl.when(mine)
                    def _():
                        out32[slot, part] = panel

                    @pl.when(jnp.logical_not(mine))
                    def _():
                        out16[slot, part] = panel.astype(out16.dtype)

                @pl.when(found < 0)
                def _():
                    store(jnp.zeros((width, width), jnp.float32))

                @pl.when(found >= 0)
                def _():
                    stacked = jnp.concatenate([factors[k, 0], factors[k, 1]], axis=1)
                    by_real = plain_product(columns[0, panel_rows, :], stacked)
                    by_imag = plain_product(columns[1, panel_rows, :], stacked)
                    real = -(by_real[:, :width] - by_imag[:, width:])
                    imag = -(by_real[:, width:] + by_imag[:, :width])
                    store(weight_real * imag + weight_imag * real)
                    both = jnp.concatenate(
                        [real.astype(jnp.bfloat16), imag.astype(jnp.bfloat16)], axis=1
                    )

                    def with_diagonal():
                        pltpu.make_async_copy(
                            matched.at[k, part], matched.at[k, part], matched_sems.at[k, part]
                        ).wait()
                        crossed_real = turned_product(matched[k, part, 0], both)
                        crossed_imag = turned_product(matched[k, part, 1], both)
                        diag_real = -(crossed_real[:, :width] - crossed_imag[:, width:])
                        diag_imag = -(crossed_real[:, width:] + crossed_imag[:, :width])
                        total[k] += weight_real * diag_imag + weight_imag * diag_real

                    if pending:
                        is_pending = functools.reduce(jnp.logical_or, [k == p for p in pending])
                        if ready:
                            pl.when(jnp.logical_not(is_pending))(with_diagonal)
                        place_in = sum(
                            jnp.where(k == p, index, 0) for index, p in enumerate(pending)
                        )

                        @pl.when(is_pending)
                        def _():
                            left[place_in, panel_rows, :] = both
                    else:
                        with_diagonal()

                out_copy(k, part, lambda copy: copy.start())

        after = pltpu.make_async_copy(total, diag_ref, diag_sem)
        after.start()
        if pending:
            keep = pltpu.make_async_copy(left, left_ref, left_sem)
            keep.start()
            keep.wait()

        @pl.loop(0, supers)
        def _(k):
            @pl.loop(0, slices)
            def _(part):
                out_copy(k, part, lambda copy: copy.wait())

        after.wait()


def lent_terms(half, known, table, places, weights, columns, tiles, parts, outputs):
    supers = tiles.shape[1]
    width = tiles.shape[5]
    depth = tiles.shape[4]
    height = columns.shape[1]
    slices = height // width
    others = columns.shape[2] // depth
    left = max(1, supers - sum(len(group) for group in CHUNKS[:known]))
    left_shape = (left, height, 2 * width)
    return pl.pallas_call(
        functools.partial(lent_kernel, half, known),
        out_shape=(
            jax.ShapeDtypeStruct((2, height, width), jnp.bfloat16),
            jax.ShapeDtypeStruct((2, height, width), jnp.float32),
            jax.ShapeDtypeStruct((supers, width, width), jnp.float32),
            jax.ShapeDtypeStruct(left_shape, jnp.bfloat16),
        ),
        in_specs=[SCALARS] * 3 + [ANYWHERE] * (2 + 3 * known + len(outputs)),
        out_specs=(ANYWHERE,) * 4,
        input_output_aliases={5 + 3 * known: 2} if outputs else {},
        scratch_shapes=[
            pltpu.VMEM(columns.shape, columns.dtype),
            pltpu.VMEM((supers, 2, others * depth, width), tiles.dtype),
            pltpu.VMEM((supers, slices, 2, 4 * depth, width), tiles.dtype),
            pltpu.VMEM((2, slices, width, width), jnp.bfloat16),
            pltpu.VMEM((2, slices, width, width), jnp.float32),
            pltpu.VMEM((supers, width, width), jnp.float32),
            pltpu.VMEM(left_shape, jnp.bfloat16),
            pltpu.SemaphoreType.DMA,
            pltpu.SemaphoreType.DMA((supers, others)),
            pltpu.SemaphoreType.DMA((supers, slices)),
            pltpu.SemaphoreType.DMA((supers, slices)),
            pltpu.SemaphoreType.DMA,
            pltpu.SemaphoreType.DMA,
        ],
        compiler_params=pltpu.CompilerParams(vmem_limit_bytes=48 * 1024 * 1024),
        cost_estimate=pl.CostEstimate(
            flops=8 * height * supers * width * others * depth,
            bytes_accessed=8 * supers * others * depth * width,
            transcendentals=0,
        ),
    )(table, places, weights, columns, tiles, *parts, *outputs)


def shards_line(inverse_pool, factor_tiles, diag_inverse, pole_weight, ancestors):
    supers = factor_tiles.shape[1]
    listed_count = factor_tiles.shape[3]
    depth = factor_tiles.shape[4]
    width = factor_tiles.shape[5]
    height = inverse_pool.shape[2]
    slices = height // width
    blocks = inverse_pool.shape[3] // width
    place = lax.axis_index("grid")
    pole = lax.axis_index("pole")
    chip = pole // 2
    core = pole % 2
    edge = jnp.logical_or(place == 0, place == 3)
    first_half = (place < 2).astype(jnp.int32)
    places = jnp.stack(
        [place, edge.astype(jnp.int32), first_half, 3 * slices * (1 - first_half), slices * first_half, chip]
    ).astype(jnp.int32)
    same = ancestors[:, :, None] == jnp.arange(blocks, dtype=jnp.int32)
    table = jnp.max(
        jnp.where(same, jnp.arange(listed_count, dtype=jnp.int32)[None, :, None], -1), axis=1
    ).astype(jnp.int32)

    def planes(places_z, pairs):
        return [(4 * z + a, 4 * z + b) for z in places_z for a, b in pairs]

    def halves(value, which, axis):
        size = value.shape[axis] // 2
        return (
            lax.dynamic_slice_in_dim(value, (1 - which) * size, size, axis),
            lax.dynamic_slice_in_dim(value, which * size, size, axis),
        )

    def joined(mine, other, which):
        return jnp.where(which == 0, jnp.concatenate([mine, other]), jnp.concatenate([other, mine]))

    near_rows = pl.pallas_call(
        near_rows_kernel,
        out_shape=jax.ShapeDtypeStruct((supers, 2, slices, depth, width), factor_tiles.dtype),
        in_specs=[SCALARS] * 2 + [ANYWHERE],
        out_specs=WHOLE,
        scratch_shapes=[pltpu.SemaphoreType.DMA((supers, slices))],
        name="near_rows",
    )(table, places, factor_tiles)
    near_rows, later = lax.optimization_barrier((near_rows, factor_tiles))
    near = lax.ppermute(near_rows, "grid", OUTWARD_Z)
    owns = [
        jnp.stack([(later if c else factor_tiles)[0, k] for k in group])
        for c, group in enumerate(CHUNKS)
    ]
    lent = []
    for half in range(2):
        packed = packed_columns(places, inverse_pool, depth, width, half, 2)
        lent.append(lax.ppermute(packed, "grid", INWARD_Z))

    parts = []
    for own in owns:
        swap = lax.ppermute(own, "grid", INWARD_Z)
        mid_near = lax.ppermute(own, "grid", MIDDLE_Z)
        mid_far = lax.ppermute(swap, "grid", MIDDLE_Z)
        end_near = lax.ppermute(mid_near, "grid", OUTWARD_Z)
        end_far = lax.ppermute(mid_far, "grid", OUTWARD_Z)
        parts.append((swap, mid_near, mid_far, end_near, end_far))

    both_axes = ("grid", "pole")
    middles = [piece for part in parts for piece in part[:3]]
    common = (table, ancestors, places, pole_weight, inverse_pool, factor_tiles)

    def node(k, role, columns, outputs):
        c = next(c for c, group in enumerate(CHUNKS) if k in group)
        swap, mid_near, mid_far, end_near, end_far = parts[c]
        wanted = (near, end_near, end_far) if role else (swap, mid_near, mid_far)
        return supernode_terms(
            k, CHUNKS[c].index(k), role, k if columns else None, *common, wanted,
            diag_inverse, columns, outputs,
        )

    def lent_node(half, known, outputs):
        return lent_terms(
            half, known, table, places, pole_weight, lent[half], factor_tiles,
            middles[: 3 * known], outputs,
        )

    lent_sent, lent_kept = [None] * 2, [None] * 2
    lent_sent[0], lent_kept[0], diag, columns = lent_node(0, 0, ())
    outer = node(0, 0, (columns,), (diag,))
    outer = node(3, 0, (columns,), outer)
    outer = node(0, 1, (), outer)
    sent_outer, kept_outer, diag = node(3, 1, (), outer)
    inner = node(1, 0, (columns,), (diag,))
    inner = node(2, 0, (columns,), inner)
    lent_sent[1], lent_kept[1], diag, _ = lent_node(1, len(CHUNKS), (inner[2],))
    sent_inner, kept_inner, diag = node(1, 1, (), (inner[0], inner[1], diag))
    sent_inner, kept_inner, diag = node(2, 1, (), (sent_inner, kept_inner, diag))

    def plus(kept, other):
        return kept + other.astype(jnp.float32)

    returned = []
    for half in range(2):
        other = lax.ppermute(lent_sent[half], both_axes, planes((1, 2), ACROSS_X))
        both = plus(lent_kept[half], other)
        mine = jnp.where(core == 0, both[0], both[1])
        yours = jnp.where(core == 0, both[1], both[0])
        mine = mine + lax.ppermute(yours, both_axes, planes((1, 2), PAIRS_Z))
        returned.append(lax.ppermute(mine.astype(jnp.bfloat16), "grid", OUTWARD_Z))

    chip_sum = plus(kept_outer, lax.ppermute(sent_outer, "pole", ACROSS_X))
    outer_sum = chip_sum + lax.ppermute(chip_sum, "pole", [(1, 0), (2, 3)])
    in_outer = jnp.logical_or(pole == 0, pole == 3)
    chip_sum = plus(kept_inner, lax.ppermute(sent_inner, "pole", ACROSS_X))
    other = lax.ppermute(chip_sum, "pole", [(0, 1), (3, 2)])
    back = jnp.concatenate(returned).astype(jnp.float32)
    base = jnp.where(edge, back, 0.0) + jnp.where(in_outer, outer_sum, 0.0)
    base, chip_sum = lax.optimization_barrier((base, chip_sum))
    panel_share = base + jnp.where(in_outer, 0.0, chip_sum + other)

    def to_quarters(value, places_z):
        sent, kept = halves(value, core, 1)
        value = kept + lax.ppermute(sent, both_axes, planes(places_z, PAIRS_Z))
        sent, kept = halves(value, chip, 1)
        return kept + lax.ppermute(sent, both_axes, planes(places_z, ACROSS_X))

    quarters = to_quarters(diag, range(4))
    own = lax.dynamic_index_in_dim(quarters, place, 0, keepdims=False)
    for shift in range(1, 4):
        sent = lax.dynamic_index_in_dim(quarters, (place + shift) % 4, 0, keepdims=False)
        own = own + lax.ppermute(sent, "grid", [(z, (z + shift) % 4) for z in range(4)])
    own = joined(own, lax.ppermute(own, "pole", ACROSS_X), chip)
    diag_share = joined(own, lax.ppermute(own, "pole", PAIRS_Z), core)
    return (panel_share, diag_share)


def solution(mesh):
    in_specs = (
        P(("ens", "pole"), None, "grid", None),
        P(("ens", "pole"), None, None, None, "grid", None),
        P(("ens", "pole"), None, "grid", None),
        P("pole", None),
        P(),
    )
    out_specs = (P(("ens", "grid"), "pole"), P(("ens", "grid"), None))

    def shards(inverse_pool, factor_tiles, diag_inverse, pole_weight, ancestors):
        groups = mesh.shape["grid"]
        poles = mesh.shape["pole"]
        supers = factor_tiles.shape[1]
        width = factor_tiles.shape[5]
        line = (
            groups == 4
            and poles == 4
            and supers == 4
            and factor_tiles.shape[4] * groups == width
            and inverse_pool.shape[2] % width == 0
            and diag_inverse.shape[2] == width
            and width % 256 == 0
        )
        if not line:
            return shards_any(inverse_pool, factor_tiles, diag_inverse, pole_weight, ancestors)
        return shards_line(inverse_pool, factor_tiles, diag_inverse, pole_weight, ancestors)

    return jax.shard_map(shards, mesh=mesh, in_specs=in_specs, out_specs=out_specs, check_vma=False)
```

```python
import functools

import jax
import jax.numpy as jnp
from jax import lax
from jax.experimental import pallas as pl
from jax.experimental.pallas import tpu as pltpu
from jax.sharding import PartitionSpec as P


def plain_product(left, right):
    return jnp.dot(left, right, preferred_element_type=jnp.float32)


def turned_product(left, right):
    return lax.dot_general(
        left, right, (((0,), (0,)), ((), ())), preferred_element_type=jnp.float32
    )


def portion_terms(rows_pair, block_index, offset, listed, factors, weights):
    tile_width = factors.shape[3]
    listed_count = factors.shape[1]
    height = rows_pair.shape[1]
    blocks = rows_pair.shape[2] // tile_width
    matches = listed == block_index

    def compute():
        chosen = rows_pair.reshape(2, height, blocks, tile_width)[:, :, listed, :].reshape(
            2, height, listed_count * tile_width
        )
        stacked = factors.reshape(2, listed_count * tile_width, tile_width)
        part_real = -(plain_product(chosen[0], stacked[0]) - plain_product(chosen[1], stacked[1]))
        part_imag = -(plain_product(chosen[0], stacked[1]) + plain_product(chosen[1], stacked[0]))
        panel_piece = weights[0] * part_imag + weights[1] * part_real
        rounded_real = part_real.astype(jnp.bfloat16)
        rounded_imag = part_imag.astype(jnp.bfloat16)
        position = jnp.sum(jnp.where(matches, jnp.arange(listed_count, dtype=jnp.int32), 0))
        matched = lax.dynamic_slice(
            factors, (jnp.int32(0), position, offset, jnp.int32(0)), (2, 1, height, tile_width)
        )[:, 0]
        diag_real = -(
            turned_product(matched[0], rounded_real) - turned_product(matched[1], rounded_imag)
        )
        diag_imag = -(
            turned_product(matched[0], rounded_imag) + turned_product(matched[1], rounded_real)
        )
        return (panel_piece, weights[0] * diag_imag + weights[1] * diag_real)

    def skipped():
        return (
            jnp.zeros((height, tile_width), jnp.float32),
            jnp.zeros((tile_width, tile_width), jnp.float32),
        )

    return lax.cond(jnp.any(matches), compute, skipped)


def rows_terms(rows_pair, row_first, listed, factors, weights):
    tile_width = factors.shape[3]
    height = rows_pair.shape[1]
    piece_rows = min(height, tile_width)
    panels = []
    diag_total = jnp.zeros((tile_width, tile_width), jnp.float32)
    for portion in range(height // piece_rows):
        row_start = row_first + portion * piece_rows
        panel_piece, diag_piece = portion_terms(
            rows_pair[:, portion * piece_rows : (portion + 1) * piece_rows],
            row_start // tile_width,
            row_start % tile_width,
            listed,
            factors,
            weights,
        )
        panels.append(panel_piece)
        diag_total = diag_total + diag_piece
    return (jnp.concatenate(panels, axis=0), diag_total)


def shards_any(inverse_pool, factor_tiles, diag_inverse, pole_weight, ancestors):
    device_index = lax.axis_index("grid")
    rows_here = inverse_pool.shape[2]
    supers = factor_tiles.shape[1]
    tile_width = factor_tiles.shape[5]
    row_slab = inverse_pool[0]
    weights = (pole_weight[0, 0], pole_weight[0, 1])
    row_first = device_index * rows_here
    own_panels = []
    diag_terms = []
    for supernode in range(supers):
        factors = lax.all_gather(factor_tiles[0, supernode], "grid", axis=2, tiled=True)
        listed = ancestors[supernode]
        own_panel, own_diag = rows_terms(row_slab, row_first, listed, factors, weights)
        diag_terms.append(own_diag)
        own_panels.append(own_panel)
    panel_rows = jnp.concatenate(own_panels, axis=1)
    panel_share = lax.psum_scatter(panel_rows, "pole", scatter_dimension=1, tiled=True)
    diag_term = jnp.stack(diag_terms, axis=0).reshape(supers * tile_width, tile_width)
    diag_local = diag_inverse[0]
    local_block = weights[0] * diag_local[1].astype(jnp.float32) + weights[1] * diag_local[
        0
    ].astype(jnp.float32)
    share_rows = local_block.shape[0]
    placed = lax.dynamic_update_slice(
        jnp.zeros_like(diag_term), local_block, (device_index * share_rows, jnp.int32(0))
    )
    spread = lax.psum_scatter(diag_term + placed, ("grid", "pole"), scatter_dimension=0, tiled=True)
    diag_share = lax.all_gather(spread, "pole", axis=0, tiled=True)
    return (panel_share, diag_share)


PAIRS_Z = [(0, 1), (1, 0), (2, 3), (3, 2)]
MIDDLE_Z = [(1, 2), (2, 1)]
OUTWARD_Z = [(1, 0), (2, 3)]
INWARD_Z = [(0, 1), (3, 2)]
ACROSS_X = [(0, 2), (2, 0), (1, 3), (3, 1)]
CHUNKS = ((0, 3), (1,), (2,))


ANYWHERE = pl.BlockSpec(memory_space=pl.ANY)
STAYING = pl.BlockSpec(memory_space=pltpu.MemorySpace.HBM)
SCALARS = pl.BlockSpec(memory_space=pltpu.SMEM)
WHOLE = pl.BlockSpec(memory_space=pltpu.VMEM)


def near_rows_kernel(table_ref, place_ref, tiles_ref, out_ref, sems):
    supers = out_ref.shape[0]
    slices = out_ref.shape[2]
    end_block = place_ref[3]

    def each(action):
        for k in range(supers):
            for part in range(slices):
                found = table_ref[k, end_block + part]

                @pl.when(found >= 0)
                def _(k=k, part=part, found=found):
                    action(
                        pltpu.make_async_copy(
                            tiles_ref.at[0, k, :, found],
                            out_ref.at[k, :, part],
                            sems.at[k, part],
                        )
                    )

    each(lambda copy: copy.start())
    each(lambda copy: copy.wait())


def pack_columns_kernel(depth, width, place_ref, pool_ref, out_ref):
    first_half = place_ref[2]
    blocks = pool_ref.shape[3] // width

    @pl.when(place_ref[1] == 1)
    def _():
        for offset, flag in ((depth, 1), (2 * depth, 0)):

            @pl.when(first_half == flag)
            def _(offset=offset):
                for part in range(2):
                    out_ref[part] = jnp.concatenate(
                        [
                            pool_ref[0, part, :, q * width + offset : q * width + offset + depth]
                            for q in range(blocks)
                        ],
                        axis=1,
                    )


def packed_columns(places, pool, depth, width, half, halves):
    height = pool.shape[2] // halves
    slices = pool.shape[2] // width
    tile = min(height, width)
    steps = height // tile
    groups = pool.shape[3] // (slices * width) - 1
    return pl.pallas_call(
        functools.partial(pack_columns_kernel, depth, width),
        out_shape=jax.ShapeDtypeStruct((2, height, groups * slices * depth), pool.dtype),
        grid_spec=pltpu.PrefetchScalarGridSpec(
            num_scalar_prefetch=1,
            grid=(steps, groups),
            in_specs=[
                pl.BlockSpec(
                    (1, 2, tile, slices * width),
                    lambda i, j, place: (0, 0, (half * steps + i) * place[1], (j + place[2]) * place[1]),
                )
            ],
            out_specs=pl.BlockSpec(
                (2, tile, slices * depth), lambda i, j, place: (0, i * place[1], j * place[1])
            ),
        ),
        cost_estimate=pl.CostEstimate(
            flops=0, bytes_accessed=3 * pool.shape[3] * height * 2, transcendentals=0
        ),
    )(places, pool)


def supernode_kernel(
    supernode,
    item_in_chunk,
    role,
    fresh,
    lent_item,
    table_ref,
    listed_ref,
    place_ref,
    weight_ref,
    pool_ref,
    tiles_ref,
    partner_ref,
    far_near_ref,
    far_far_ref,
    local_ref,
    *refs,
):
    columns_ref = None
    if lent_item is not None:
        columns_ref, *refs = refs
    diag_in_ref = refs[0] if fresh else refs[2]
    refs = refs[1:] if fresh else refs[3:]
    (
        sent_ref,
        kept_ref,
        diag_ref,
        factors,
        rows,
        out16,
        out32,
        total,
        columns,
        factor_sems,
        near_sems,
        row_sems,
        out_sems,
        diag_sem,
        column_sem,
    ) = refs
    width = total.shape[0]
    listed_count = factors.shape[0]
    slices = rows.shape[0]
    depth = tiles_ref.shape[4]
    place = place_ref[0]
    first_half = place_ref[2]
    end_block = place_ref[3]
    keeps = place_ref[5] == supernode // 2
    odd = lax.rem(place, 2)

    own_base = 2 * (1 - first_half)
    far_base = 2 * first_half
    near_slot = 1 - first_half
    near_start = pl.multiple_of((1 - odd + own_base) * depth, depth)
    pieces = [
        (tiles_ref.at[0, supernode], odd + own_base),
        (far_near_ref.at[item_in_chunk], near_slot + far_base),
        (far_far_ref.at[item_in_chunk], 1 - near_slot + far_base),
    ]
    if not role:
        pieces.append((partner_ref.at[item_in_chunk], 1 - odd + own_base))

    def each_piece(action):
        for number, (source, slot) in enumerate(pieces):
            start = pl.multiple_of(slot * depth, depth)
            for part in range(2):
                action(
                    pltpu.make_async_copy(
                        source.at[part],
                        factors.at[:, pl.ds(start, depth), pl.ds(part * width, width)],
                        factor_sems.at[number, part],
                    )
                )

    def each_near(action):
        @pl.loop(0, slices)
        def _(part):
            found = table_ref[supernode, place * slices + part]

            @pl.when(found >= 0)
            def _():
                for half in range(2):
                    action(
                        pltpu.make_async_copy(
                            partner_ref.at[supernode, half, part],
                            factors.at[found, pl.ds(near_start, depth), pl.ds(half * width, width)],
                            near_sems.at[part, half],
                        )
                    )

    def store(part, panel):
        @pl.when(keeps)
        def _():
            out32[part] = panel

        @pl.when(jnp.logical_not(keeps))
        def _():
            out16[part] = panel.astype(out16.dtype)

    def out_copy(part, action):
        panel_rows = pl.ds(pl.multiple_of(part * width, width), width)

        @pl.when(keeps)
        def _():
            action(
                pltpu.make_async_copy(out32.at[part], kept_ref.at[panel_rows, :], out_sems.at[part])
            )

        @pl.when(jnp.logical_not(keeps))
        def _():
            action(
                pltpu.make_async_copy(out16.at[part], sent_ref.at[panel_rows, :], out_sems.at[part])
            )

    @pl.when(place_ref[1] == role)
    def _():
        each_piece(lambda copy: copy.start())
        if role:
            each_near(lambda copy: copy.start())
        else:
            before = pltpu.make_async_copy(diag_in_ref.at[supernode], total, diag_sem)
            before.start()

        @pl.loop(0, slices)
        def _(part):
            @pl.when(table_ref[supernode, place * slices + part] >= 0)
            def _():
                @pl.loop(0, listed_count)
                def _(item):
                    column = pl.multiple_of(listed_ref[supernode, item] * width, width)
                    start = pl.multiple_of(part * width, width)
                    pltpu.make_async_copy(
                        pool_ref.at[0, :, pl.ds(start, width), pl.ds(column, width)],
                        rows.at[part, :, :, pl.ds(pl.multiple_of(item * width, width), width)],
                        row_sems.at[part],
                    ).start()

        if columns_ref is not None:
            lent_copy = pltpu.make_async_copy(columns_ref.at[lent_item], columns, column_sem)
            lent_copy.start()
        if role:

            @pl.loop(0, listed_count)
            def _(item):
                block = listed_ref[supernode, item]

                @pl.when(jnp.logical_or(block < end_block, block >= end_block + slices))
                def _():
                    factors[item, pl.ds(near_start, depth), :] = jnp.zeros(
                        (depth, 2 * width), factors.dtype
                    )

            total[...] = jnp.zeros(total.shape, total.dtype)
        else:
            before.wait()

        weight_real = weight_ref[0, 0]
        weight_imag = weight_ref[0, 1]

        @pl.when(place == supernode)
        def _():
            total[...] += weight_real * local_ref[0, 1].astype(jnp.float32) + weight_imag * local_ref[
                0, 0
            ].astype(jnp.float32)

        def add_diagonal(found, both):
            crossed = turned_product(factors[found], both)
            diag_real = -(crossed[:width, :width] - crossed[width:, width:])
            diag_imag = -(crossed[:width, width:] + crossed[width:, :width])
            total[...] += weight_real * diag_imag + weight_imag * diag_real

        each_piece(lambda copy: copy.wait())
        if role:
            each_near(lambda copy: copy.wait())

        @pl.loop(0, slices)
        def _(part):
            found = table_ref[supernode, place * slices + part]

            @pl.when(found < 0)
            def _():
                store(part, jnp.zeros((width, width), jnp.float32))

            @pl.when(found >= 0)
            def _():
                pltpu.make_async_copy(
                    pool_ref.at[0, :, pl.ds(0, width), pl.ds(0, listed_count * width)],
                    rows.at[part],
                    row_sems.at[part],
                ).wait()
                stacked = factors[...].reshape(listed_count * 4 * depth, 2 * width)
                by_real = plain_product(rows[part, 0], stacked)
                by_imag = plain_product(rows[part, 1], stacked)
                real = -(by_real[:, :width] - by_imag[:, width:])
                imag = -(by_real[:, width:] + by_imag[:, :width])
                store(part, weight_real * imag + weight_imag * real)
                add_diagonal(
                    found,
                    jnp.concatenate([real.astype(jnp.bfloat16), imag.astype(jnp.bfloat16)], axis=1),
                )

            out_copy(part, lambda copy: copy.start())

        if columns_ref is not None:
            lent_copy.wait()

            @pl.loop(0, columns.shape[0] // width)
            def _(part):
                found = table_ref[supernode, end_block + part]

                @pl.when(found >= 0)
                def _():
                    start = pl.multiple_of(part * width, width)
                    add_diagonal(found, columns[pl.ds(start, width), :])

        after = pltpu.make_async_copy(total, diag_ref.at[supernode], diag_sem)
        after.start()

        @pl.loop(0, slices)
        def _(part):
            out_copy(part, lambda copy: copy.wait())

        after.wait()


def supernode_terms(
    k, item, role, lent_item, table, listed, places, weights, pool, tiles, parts, local, columns, outputs
):
    width = tiles.shape[5]
    depth = tiles.shape[4]
    listed_count = tiles.shape[3]
    height = pool.shape[2]
    slices = height // width
    fresh = len(outputs) == 1
    first = 10 + len(columns)
    aliases = {first: 2} if fresh else {first + 2: 2, first: 0, first + 1: 1}
    lent_height = columns[0].shape[1] if columns else width
    return pl.pallas_call(
        functools.partial(supernode_kernel, k, item, role, fresh, lent_item),
        out_shape=(
            jax.ShapeDtypeStruct((height, width), jnp.bfloat16),
            jax.ShapeDtypeStruct((height, width), jnp.float32),
            jax.ShapeDtypeStruct((tiles.shape[1], width, width), jnp.float32),
        ),
        in_specs=[SCALARS] * 4
        + [STAYING] * 2
        + [ANYWHERE] * 3
        + [WHOLE]
        + [ANYWHERE] * (len(columns) + len(outputs)),
        out_specs=(ANYWHERE, ANYWHERE, ANYWHERE),
        input_output_aliases=aliases,
        scratch_shapes=[
            pltpu.VMEM((listed_count, 4 * depth, 2 * width), jnp.bfloat16),
            pltpu.VMEM((slices, 2, width, listed_count * width), jnp.bfloat16),
            pltpu.VMEM((slices, width, width), jnp.bfloat16),
            pltpu.VMEM((slices, width, width), jnp.float32),
            pltpu.VMEM((width, width), jnp.float32),
            pltpu.VMEM((lent_height, 2 * width), jnp.bfloat16),
            pltpu.SemaphoreType.DMA((4, 2)),
            pltpu.SemaphoreType.DMA((slices, 2)),
            pltpu.SemaphoreType.DMA((slices,)),
            pltpu.SemaphoreType.DMA((slices,)),
            pltpu.SemaphoreType.DMA,
            pltpu.SemaphoreType.DMA,
        ],
        compiler_params=pltpu.CompilerParams(vmem_limit_bytes=40 * 1024 * 1024),
        cost_estimate=pl.CostEstimate(
            flops=8 * height * width * width * listed_count,
            bytes_accessed=6 * height * width * listed_count,
            transcendentals=0,
        ),
    )(table, listed, places, weights, pool, tiles, *parts, local, *columns, *outputs)


def lent_kernel(
    half,
    known,
    table_ref,
    place_ref,
    weight_ref,
    columns_ref,
    tiles_ref,
    *refs,
):
    part_refs = [refs[3 * c : 3 * c + 3] for c in range(known)]
    refs = refs[3 * known :]
    diag_in_ref = None
    if half:
        diag_in_ref, *refs = refs
    (
        sent_ref,
        kept_ref,
        diag_ref,
        left_ref,
        columns,
        factors,
        matched,
        out16,
        out32,
        total,
        left,
        column_sem,
        factor_sems,
        matched_sems,
        out_sems,
        diag_sem,
        left_sem,
    ) = refs
    supers, width, _ = total.shape
    depth = tiles_ref.shape[4]
    slices = columns.shape[1] // width
    others = factors.shape[2] // depth
    place = place_ref[0]
    edge = place_ref[1]
    first_half = place_ref[2]
    end_block = place_ref[3]
    other_first = place_ref[4]
    chip = place_ref[5]
    weight_real = weight_ref[0, 0]
    weight_imag = weight_ref[0, 1]
    first_block = end_block + half * slices
    ready = [k for group in CHUNKS[:known] for k in group]
    pending = [k for k in range(supers) if k not in ready]

    @pl.when(edge == 0)
    def _():
        whole = pltpu.make_async_copy(columns_ref, columns, column_sem)
        whole.start()
        if half:
            before = pltpu.make_async_copy(diag_in_ref, total, diag_sem)
            before.start()

        @pl.loop(0, supers)
        def _(k):
            @pl.loop(0, others)
            def _(other):
                found = table_ref[k, other_first + other]
                span = pl.ds(pl.multiple_of(other * depth, depth), depth)

                @pl.when(found >= 0)
                def _():
                    pltpu.make_async_copy(
                        tiles_ref.at[0, k, :, found],
                        factors.at[k, :, span, :],
                        factor_sems.at[k, other],
                    ).start()

                @pl.when(found < 0)
                def _():
                    factors[k, :, span, :] = jnp.zeros((2, depth, width), factors.dtype)

        for chunk, group in enumerate(CHUNKS[:known]):
            swap_ref, near_ref, far_ref = part_refs[chunk]
            for item, k in enumerate(group):

                @pl.loop(0, slices)
                def _(part, k=k, item=item, swap_ref=swap_ref, near_ref=near_ref, far_ref=far_ref):
                    found = table_ref[k, first_block + part]

                    @pl.when(found >= 0)
                    def _():
                        for source, slot in (
                            (tiles_ref.at[0, k], place),
                            (swap_ref.at[item], 3 * (1 - first_half)),
                            (near_ref.at[item], 1 + first_half),
                            (far_ref.at[item], 3 * first_half),
                        ):
                            start = pl.multiple_of(slot * depth, depth)
                            pltpu.make_async_copy(
                                source.at[:, found],
                                matched.at[k, part, :, pl.ds(start, depth), :],
                                matched_sems.at[k, part],
                            ).start()

        if half:
            before.wait()
        else:
            total[...] = jnp.zeros(total.shape, total.dtype)
        whole.wait()

        def out_copy(k, part, action):
            panel_rows = pl.ds(pl.multiple_of(part * width, width), width)
            slot = lax.rem(k, 2)

            @pl.when(chip == k // 2)
            def _():
                action(
                    pltpu.make_async_copy(
                        out32.at[slot, part], kept_ref.at[slot, panel_rows, :], out_sems.at[k, part]
                    )
                )

            @pl.when(chip != k // 2)
            def _():
                action(
                    pltpu.make_async_copy(
                        out16.at[slot, part], sent_ref.at[slot, panel_rows, :], out_sems.at[k, part]
                    )
                )

        @pl.loop(0, supers)
        def _(k):
            @pl.loop(0, others)
            def _(other):
                span = pl.ds(pl.multiple_of(other * depth, depth), depth)

                @pl.when(table_ref[k, other_first + other] >= 0)
                def _():
                    pltpu.make_async_copy(
                        factors.at[k, :, span, :], factors.at[k, :, span, :], factor_sems.at[k, other]
                    ).wait()

            slot = lax.rem(k, 2)
            mine = chip == k // 2

            @pl.loop(0, slices)
            def _(part):
                found = table_ref[k, first_block + part]
                panel_rows = pl.ds(pl.multiple_of(part * width, width), width)

                def store(panel):
                    @pl.when(mine)
                    def _():
                        out32[slot, part] = panel

                    @pl.when(jnp.logical_not(mine))
                    def _():
                        out16[slot, part] = panel.astype(out16.dtype)

                @pl.when(found < 0)
                def _():
                    store(jnp.zeros((width, width), jnp.float32))

                @pl.when(found >= 0)
                def _():
                    stacked = jnp.concatenate([factors[k, 0], factors[k, 1]], axis=1)
                    by_real = plain_product(columns[0, panel_rows, :], stacked)
                    by_imag = plain_product(columns[1, panel_rows, :], stacked)
                    real = -(by_real[:, :width] - by_imag[:, width:])
                    imag = -(by_real[:, width:] + by_imag[:, :width])
                    store(weight_real * imag + weight_imag * real)
                    both = jnp.concatenate(
                        [real.astype(jnp.bfloat16), imag.astype(jnp.bfloat16)], axis=1
                    )

                    def with_diagonal():
                        pltpu.make_async_copy(
                            matched.at[k, part], matched.at[k, part], matched_sems.at[k, part]
                        ).wait()
                        crossed_real = turned_product(matched[k, part, 0], both)
                        crossed_imag = turned_product(matched[k, part, 1], both)
                        diag_real = -(crossed_real[:, :width] - crossed_imag[:, width:])
                        diag_imag = -(crossed_real[:, width:] + crossed_imag[:, :width])
                        total[k] += weight_real * diag_imag + weight_imag * diag_real

                    if pending:
                        is_pending = functools.reduce(jnp.logical_or, [k == p for p in pending])
                        if ready:
                            pl.when(jnp.logical_not(is_pending))(with_diagonal)
                        place_in = sum(
                            jnp.where(k == p, index, 0) for index, p in enumerate(pending)
                        )

                        @pl.when(is_pending)
                        def _():
                            left[place_in, panel_rows, :] = both
                    else:
                        with_diagonal()

                out_copy(k, part, lambda copy: copy.start())

        after = pltpu.make_async_copy(total, diag_ref, diag_sem)
        after.start()
        if pending:
            keep = pltpu.make_async_copy(left, left_ref, left_sem)
            keep.start()
            keep.wait()

        @pl.loop(0, supers)
        def _(k):
            @pl.loop(0, slices)
            def _(part):
                out_copy(k, part, lambda copy: copy.wait())

        after.wait()


def lent_terms(half, known, table, places, weights, columns, tiles, parts, outputs):
    supers = tiles.shape[1]
    width = tiles.shape[5]
    depth = tiles.shape[4]
    height = columns.shape[1]
    slices = height // width
    others = columns.shape[2] // depth
    left = max(1, supers - sum(len(group) for group in CHUNKS[:known]))
    left_shape = (left, height, 2 * width)
    return pl.pallas_call(
        functools.partial(lent_kernel, half, known),
        out_shape=(
            jax.ShapeDtypeStruct((2, height, width), jnp.bfloat16),
            jax.ShapeDtypeStruct((2, height, width), jnp.float32),
            jax.ShapeDtypeStruct((supers, width, width), jnp.float32),
            jax.ShapeDtypeStruct(left_shape, jnp.bfloat16),
        ),
        in_specs=[SCALARS] * 3 + [ANYWHERE] * (2 + 3 * known + len(outputs)),
        out_specs=(ANYWHERE,) * 4,
        input_output_aliases={5 + 3 * known: 2} if outputs else {},
        scratch_shapes=[
            pltpu.VMEM(columns.shape, columns.dtype),
            pltpu.VMEM((supers, 2, others * depth, width), tiles.dtype),
            pltpu.VMEM((supers, slices, 2, 4 * depth, width), tiles.dtype),
            pltpu.VMEM((2, slices, width, width), jnp.bfloat16),
            pltpu.VMEM((2, slices, width, width), jnp.float32),
            pltpu.VMEM((supers, width, width), jnp.float32),
            pltpu.VMEM(left_shape, jnp.bfloat16),
            pltpu.SemaphoreType.DMA,
            pltpu.SemaphoreType.DMA((supers, others)),
            pltpu.SemaphoreType.DMA((supers, slices)),
            pltpu.SemaphoreType.DMA((supers, slices)),
            pltpu.SemaphoreType.DMA,
            pltpu.SemaphoreType.DMA,
        ],
        compiler_params=pltpu.CompilerParams(vmem_limit_bytes=40 * 1024 * 1024),
        cost_estimate=pl.CostEstimate(
            flops=8 * height * supers * width * others * depth,
            bytes_accessed=8 * supers * others * depth * width,
            transcendentals=0,
        ),
    )(table, places, weights, columns, tiles, *parts, *outputs)


def shards_line(inverse_pool, factor_tiles, diag_inverse, pole_weight, ancestors):
    supers = factor_tiles.shape[1]
    listed_count = factor_tiles.shape[3]
    depth = factor_tiles.shape[4]
    width = factor_tiles.shape[5]
    height = inverse_pool.shape[2]
    slices = height // width
    blocks = inverse_pool.shape[3] // width
    place = lax.axis_index("grid")
    pole = lax.axis_index("pole")
    chip = pole // 2
    core = pole % 2
    edge = jnp.logical_or(place == 0, place == 3)
    first_half = (place < 2).astype(jnp.int32)
    places = jnp.stack(
        [place, edge.astype(jnp.int32), first_half, 3 * slices * (1 - first_half), slices * first_half, chip]
    ).astype(jnp.int32)
    same = ancestors[:, :, None] == jnp.arange(blocks, dtype=jnp.int32)
    table = jnp.max(
        jnp.where(same, jnp.arange(listed_count, dtype=jnp.int32)[None, :, None], -1), axis=1
    ).astype(jnp.int32)

    def planes(places_z, pairs):
        return [(4 * z + a, 4 * z + b) for z in places_z for a, b in pairs]

    def halves(value, which, axis):
        size = value.shape[axis] // 2
        return (
            lax.dynamic_slice_in_dim(value, (1 - which) * size, size, axis),
            lax.dynamic_slice_in_dim(value, which * size, size, axis),
        )

    def joined(mine, other, which):
        return jnp.where(which == 0, jnp.concatenate([mine, other]), jnp.concatenate([other, mine]))

    near_rows = pl.pallas_call(
        near_rows_kernel,
        out_shape=jax.ShapeDtypeStruct((supers, 2, slices, depth, width), factor_tiles.dtype),
        in_specs=[SCALARS] * 2 + [ANYWHERE],
        out_specs=WHOLE,
        scratch_shapes=[pltpu.SemaphoreType.DMA((supers, slices))],
        name="near_rows",
    )(table, places, factor_tiles)
    near_rows, later = lax.optimization_barrier((near_rows, factor_tiles))
    near = lax.ppermute(near_rows, "grid", OUTWARD_Z)
    owns = [
        jnp.stack([(later if c else factor_tiles)[0, k] for k in group])
        for c, group in enumerate(CHUNKS)
    ]
    lent = []
    for half in range(2):
        packed = packed_columns(places, inverse_pool, depth, width, half, 2)
        lent.append(lax.ppermute(packed, "grid", INWARD_Z))

    parts = []
    for own in owns:
        swap = lax.ppermute(own, "grid", INWARD_Z)
        mid_near = lax.ppermute(own, "grid", MIDDLE_Z)
        mid_far = lax.ppermute(swap, "grid", MIDDLE_Z)
        end_near = lax.ppermute(mid_near, "grid", OUTWARD_Z)
        end_far = lax.ppermute(mid_far, "grid", OUTWARD_Z)
        parts.append((swap, mid_near, mid_far, end_near, end_far))

    both_axes = ("grid", "pole")
    middles = [piece for part in parts for piece in part[:3]]
    common = (table, ancestors, places, pole_weight, inverse_pool, factor_tiles)

    def node(k, role, columns, outputs):
        c = next(c for c, group in enumerate(CHUNKS) if k in group)
        swap, mid_near, mid_far, end_near, end_far = parts[c]
        wanted = (near, end_near, end_far) if role else (swap, mid_near, mid_far)
        return supernode_terms(
            k, CHUNKS[c].index(k), role, k if columns else None, *common, wanted,
            diag_inverse, columns, outputs,
        )

    def lent_node(half, known, outputs):
        return lent_terms(
            half, known, table, places, pole_weight, lent[half], factor_tiles,
            middles[: 3 * known], outputs,
        )

    lent_sent, lent_kept = [None] * 2, [None] * 2
    lent_sent[0], lent_kept[0], diag, columns = lent_node(0, 0, ())
    outer = node(0, 0, (columns,), (diag,))
    outer = node(3, 0, (columns,), outer)
    outer = node(0, 1, (), outer)
    sent_outer, kept_outer, diag = node(3, 1, (), outer)
    *inner, diag = node(1, 0, (columns,), (diag,))
    lent_sent[1], lent_kept[1], diag, _ = lent_node(1, len(CHUNKS), (diag,))
    inner = node(2, 0, (columns,), (*inner, diag))
    inner = node(1, 1, (), inner)
    *inner, diag = node(2, 1, (), inner)
    sent_inner, kept_inner = inner

    def plus(kept, other):
        return kept + other.astype(jnp.float32)

    returned = []
    for half in range(2):
        other = lax.ppermute(lent_sent[half], both_axes, planes((1, 2), ACROSS_X))
        both = plus(lent_kept[half], other)
        mine = jnp.where(core == 0, both[0], both[1])
        yours = jnp.where(core == 0, both[1], both[0])
        mine = mine + lax.ppermute(yours, both_axes, planes((1, 2), PAIRS_Z))
        returned.append(lax.ppermute(mine.astype(jnp.bfloat16), "grid", OUTWARD_Z))

    chip_sum = plus(kept_outer, lax.ppermute(sent_outer, "pole", ACROSS_X))
    outer_sum = chip_sum + lax.ppermute(chip_sum, "pole", [(1, 0), (2, 3)])
    in_outer = jnp.logical_or(pole == 0, pole == 3)
    chip_sum = plus(kept_inner, lax.ppermute(sent_inner, "pole", ACROSS_X))
    other = lax.ppermute(chip_sum, "pole", [(0, 1), (3, 2)])
    back = jnp.concatenate(returned).astype(jnp.float32)
    base = jnp.where(edge, back, 0.0) + jnp.where(in_outer, outer_sum, 0.0)
    base, chip_sum = lax.optimization_barrier((base, chip_sum))
    panel_share = base + jnp.where(in_outer, 0.0, chip_sum + other)

    def to_quarters(value, places_z):
        sent, kept = halves(value, core, 1)
        value = kept + lax.ppermute(sent, both_axes, planes(places_z, PAIRS_Z))
        sent, kept = halves(value, chip, 1)
        return kept + lax.ppermute(sent, both_axes, planes(places_z, ACROSS_X))

    quarters = to_quarters(diag, range(4))
    own = lax.dynamic_index_in_dim(quarters, place, 0, keepdims=False)
    for shift in range(1, 4):
        sent = lax.dynamic_index_in_dim(quarters, (place + shift) % 4, 0, keepdims=False)
        own = own + lax.ppermute(sent, "grid", [(z, (z + shift) % 4) for z in range(4)])
    own = joined(own, lax.ppermute(own, "pole", ACROSS_X), chip)
    diag_share = joined(own, lax.ppermute(own, "pole", PAIRS_Z), core)
    return (panel_share, diag_share)


def solution(mesh):
    in_specs = (
        P(("ens", "pole"), None, "grid", None),
        P(("ens", "pole"), None, None, None, "grid", None),
        P(("ens", "pole"), None, "grid", None),
        P("pole", None),
        P(),
    )
    out_specs = (P(("ens", "grid"), "pole"), P(("ens", "grid"), None))

    def shards(inverse_pool, factor_tiles, diag_inverse, pole_weight, ancestors):
        groups = mesh.shape["grid"]
        poles = mesh.shape["pole"]
        supers = factor_tiles.shape[1]
        width = factor_tiles.shape[5]
        line = (
            groups == 4
            and poles == 4
            and supers == 4
            and factor_tiles.shape[4] * groups == width
            and inverse_pool.shape[2] % width == 0
            and diag_inverse.shape[2] == width
            and width % 256 == 0
        )
        if not line:
            return shards_any(inverse_pool, factor_tiles, diag_inverse, pole_weight, ancestors)
        return shards_line(inverse_pool, factor_tiles, diag_inverse, pole_weight, ancestors)

    return jax.shard_map(shards, mesh=mesh, in_specs=in_specs, out_specs=out_specs, check_vma=False)
```
